512 devices in a mesh: seq: 64 (over y, z), head: 8 (over x, core).
Axes of the slice: x: 4, y: 8, z: 8, core: 2. Of those that a mesh axis runs over, the one named last changes fastest.
Arguments:
- layer_input_rows: bfloat16 [8192, 4096], P('seq', 'head'), may hold values from -6 to 6
- filter_input_channels: bfloat16 [8192, 8192], P('seq', 'head'), may hold values from -6 to 6
- gate_input_channels: bfloat16 [8192, 8192], P('seq', 'head'), may hold values from -6 to 6
- state_input_vectors: bfloat16 [8192, 128], P('seq'), may hold values from -3 to 3
- state_output_vectors: bfloat16 [8192, 128], P('seq'), may hold values from -3 to 3
- decay_logarithm: float32 [8192, 64], P('seq', 'head'), may hold values from -0.7 to 0, as said below
- filter_tap_weight: bfloat16 [4, 8192], P(None, 'head'), may hold values from -3 to 3
- head_skip_gain: float32 [64], P('head'), may hold values from 0.5 to 1.5
- gated_norm_gain: float32 [8192], P('head'), may hold values from 0.1 to 1.9
- adapter_down_in: bfloat16 [4096, 32], P('head'), may hold values from -0.09375 to 0.09375
- adapter_up_in: bfloat16 [2, 32, 8192], P(None, None, 'head'), may hold values from -1 to 1
- adapter_down_out: bfloat16 [8192, 32], P('head'), may hold values from -0.0625 to 0.0625
- adapter_up_out: bfloat16 [32, 4096], P(None, 'head'), may hold values from -1 to 1
- output_gradient: bfloat16 [8192, 4096], P('seq', 'head'), may hold values from -6 to 6
- base_path_gradient: bfloat16 [8192, 8192], P('seq', 'head'), may hold values from -6 to 6
Outputs:
- grad_conv_in: bfloat16 [8192, 8192], P('seq', 'head')
- grad_gate_in: bfloat16 [8192, 8192], P('seq', 'head')
- grad_state_b: float32 [8192, 128], P(('seq', 'head'))
- grad_state_c: float32 [8192, 128], P(('seq', 'head'))
- grad_log_decay: float32 [8192, 64], P('seq', 'head')
- grad_layer_in: bfloat16 [8192, 4096], P('seq', 'head')
- grad_lora_a_in: float32 [4096, 32], P('head')
- grad_lora_b_in: float32 [2, 32, 8192], P(None, None, 'head')
- grad_lora_a_out: float32 [8192, 32], P('head')
- grad_lora_b_out: float32 [32, 4096], P(None, 'head')
The draws below stay inside these ranges and needn't reach their ends.
Inputs may be any that keep to these rules, and one draw needn't show every extreme that they name: `decay_logarithm`: each entry is the logarithm of a decay factor between 0 and 1.
All inputs are finite; a program needn't handle non-finite values.
Results may differ from the reference program's by a relative error of at most 0.0017.
Values may be sent and summed in bfloat16 or wider, within the bound.
A program may use at most 128 MiB of HBM per device.

```python
import math
import jax
import jax.numpy as jnp
from jax import lax

MODEL_WIDTH = 4096
HEAD_TOTAL = 64
HDIM = 128
NSTATE = 128
KCONV = 4
ADAPTER_RANK = 32
BLOCK = 256
TOK_DEV = 128
TOKEN_TOTAL = 8192
CHANNEL_TOTAL = 8192


def draw_decay_logarithm(key, part):
    sequence_batch = jax.random.split(jax.random.fold_in(key, 17), 8)
    quick_share = 0.2
    middle_share = 0.3
    kind_draw = jax.random.uniform(sequence_batch[0], (HEAD_TOTAL,))
    quick = kind_draw < quick_share
    middle = jnp.logical_and(kind_draw >= quick_share, kind_draw < quick_share + middle_share)
    quick_rate = 1.0 / jax.random.uniform(sequence_batch[1], (HEAD_TOTAL,), minval=30.0, maxval=50.0)
    middle_rate = jax.random.uniform(sequence_batch[7], (HEAD_TOTAL,), minval=0.04, maxval=0.13) / TOK_DEV
    slow_rate = jax.random.uniform(sequence_batch[2], (HEAD_TOTAL,), minval=0.15, maxval=0.35) / TOKEN_TOTAL
    speeds = jnp.where(quick, quick_rate, jnp.where(middle, middle_rate, slow_rate))
    shard_count = TOKEN_TOTAL // TOK_DEV
    shard_factor = jnp.exp(jax.random.uniform(sequence_batch[3], (shard_count, 1, HEAD_TOTAL), minval=math.log(0.5), maxval=math.log(2.0)))
    cell_factor = jax.random.uniform(sequence_batch[4], (shard_count, TOK_DEV, HEAD_TOTAL), minval=0.5, maxval=1.5)
    logarithm_increments = -(speeds[None, None, :] * shard_factor * cell_factor).reshape(TOKEN_TOTAL, HEAD_TOTAL)
    spike_index = jax.random.randint(sequence_batch[5], (2,), 0, TOKEN_TOTAL)
    spike_length = jnp.log(jax.random.uniform(sequence_batch[6], (2, HEAD_TOTAL), minval=0.6, maxval=0.8))
    token_position = jnp.arange(TOKEN_TOTAL)
    first_spike_token = (token_position == spike_index[0]).astype(jnp.float32)[:, None]
    second_spike_token = (token_position == spike_index[1]).astype(jnp.float32)[:, None]
    logarithm_increments = logarithm_increments + first_spike_token * spike_length[0][None, :] + second_spike_token * spike_length[1][None, :]
    return logarithm_increments.astype(jnp.float32)


def block_levels(own_key, dims, pieces, smallest, top_value):
    gain, own = 1.0, jax.random.fold_in(own_key, 6)
    for axis_at, shards_of in pieces:
        steps = jnp.exp(jax.random.uniform(jax.random.fold_in(own, axis_at), (shards_of,), jnp.float32, smallest / len(pieces), top_value / len(pieces)))
        gain = gain * jnp.repeat(steps, dims[axis_at] // shards_of).reshape([-1 if axis == axis_at else 1 for axis in range(len(dims))])
    return gain


def centred(stream_key, extent, width, most, cuts=(), kind=jnp.bfloat16):
    array = width * jax.random.normal(stream_key, extent, jnp.float32)
    if cuts:
        array = array * block_levels(stream_key, extent, cuts, -0.22, 0.18)
    return jnp.clip(array, -most, most).astype(kind)


def setup_inputs(seed: int = 0) -> dict:
    arg_keys = jax.random.split(jax.random.key(seed), 16)
    return {
        "layer_input_rows": centred(arg_keys[0], (TOKEN_TOTAL, MODEL_WIDTH), 1.0, 6.0, ((0, 64), (1, 8))),
        "filter_input_channels": centred(arg_keys[1], (TOKEN_TOTAL, CHANNEL_TOTAL), 1.0, 6.0, ((0, 64), (1, 8))),
        "gate_input_channels": centred(arg_keys[2], (TOKEN_TOTAL, CHANNEL_TOTAL), 1.0, 6.0, ((0, 64), (1, 8))),
        "state_input_vectors": centred(arg_keys[3], (TOKEN_TOTAL, NSTATE), 0.5, 3.0, ((0, 64),)),
        "state_output_vectors": centred(arg_keys[4], (TOKEN_TOTAL, NSTATE), 0.5, 3.0, ((0, 64),)),
        "decay_logarithm": draw_decay_logarithm(jax.random.fold_in(arg_keys[15], 71), 0),
        "filter_tap_weight": centred(arg_keys[6], (KCONV, CHANNEL_TOTAL), KCONV ** -0.5, 3.0, ((1, 8),)),
        "head_skip_gain": jnp.clip(0.5 + 1.0 * jax.random.uniform(arg_keys[7], (HEAD_TOTAL,), jnp.float32) ** block_levels(arg_keys[7], (HEAD_TOTAL,), ((0, 8),), -0.2, 0.2), 0.5, 1.5),
        "gated_norm_gain": jnp.clip(1.0 + 0.18 * jax.random.normal(arg_keys[8], (CHANNEL_TOTAL,), jnp.float32), 0.1, 1.9),
        "adapter_down_in": centred(arg_keys[9], (MODEL_WIDTH, ADAPTER_RANK), MODEL_WIDTH ** -0.5, 0.09375, ((0, 8),)),
        "adapter_up_in": centred(arg_keys[10], (2, ADAPTER_RANK, CHANNEL_TOTAL), ADAPTER_RANK ** -0.5, 1.0, ((2, 8),)),
        "adapter_down_out": centred(arg_keys[11], (CHANNEL_TOTAL, ADAPTER_RANK), CHANNEL_TOTAL ** -0.5, 0.0625, ((0, 8),)),
        "adapter_up_out": centred(arg_keys[12], (ADAPTER_RANK, MODEL_WIDTH), ADAPTER_RANK ** -0.5, 1.0, ((1, 8),)),
        "output_gradient": centred(arg_keys[13], (TOKEN_TOTAL, MODEL_WIDTH), 1.0, 6.0, ((0, 64), (1, 8))),
        "base_path_gradient": centred(arg_keys[14], (TOKEN_TOTAL, CHANNEL_TOTAL), 1.0, 6.0, ((0, 64), (1, 8))),
    }


PRECISE_PRODUCT = lax.Precision.HIGHEST
ADAPTER_SCALE = 2.0
NORM_EPS = 1e-05

def block_pass(activated, b_float, c_float, logarithm_increments, start_state, block_rows):
    tok_rows, head_count, head_width = activated.shape
    block_count = tok_rows // block_rows
    state_width = b_float.shape[1]
    causal = (jnp.arange(block_rows)[:, None] >= jnp.arange(block_rows)[None, :])[None, :, :]

    def advance(carried_state, block_items):
        x_block, b_block, c_block, l_block = block_items
        cum_decay = jnp.cumsum(l_block, axis=0)
        cum_heads = cum_decay.T
        decay_gap = jnp.where(causal, cum_heads[:, :, None] - cum_heads[:, None, :], 0.0)
        decays = jnp.where(causal, jnp.exp(decay_gap), 0.0)
        scores = jnp.dot(c_block, b_block.T, precision=PRECISE_PRODUCT)
        weights = decays * scores[None, :, :]
        inner_out = jnp.einsum('hts,shp->thp', weights, x_block, precision=PRECISE_PRODUCT)
        outer_out = jnp.exp(cum_decay)[:, :, None] * jnp.einsum('tn,hnp->thp', c_block, carried_state, precision=PRECISE_PRODUCT)
        to_end = jnp.exp(cum_decay[-1][None, :] - cum_decay)
        fresh_state = jnp.einsum('sn,shp->hnp', b_block, x_block * to_end[:, :, None], precision=PRECISE_PRODUCT)
        next_state = jnp.exp(cum_decay[-1])[:, None, None] * carried_state + fresh_state
        return (next_state, inner_out + outer_out)
    block_items = (activated.reshape(block_count, block_rows, head_count, head_width), b_float.reshape(block_count, block_rows, state_width), c_float.reshape(block_count, block_rows, state_width), logarithm_increments.reshape(block_count, block_rows, head_count))
    end_state, outputs = lax.scan(jax.checkpoint(advance), start_state, block_items)
    return (outputs.reshape(tok_rows, head_count, head_width), end_state)

def mixer_forward(conv_float, gate_float, b_float, c_float, logarithm_increments, filter_tap_weight, head_skip_gain, gated_norm_gain):
    tok_rows = conv_float.shape[0]
    padded = jnp.concatenate([jnp.zeros((KCONV - 1, CHANNEL_TOTAL), jnp.float32), conv_float], axis=0)
    taps = filter_tap_weight.astype(jnp.float32)
    pre_act = padded[0:tok_rows] * taps[0][None, :]
    for offset in range(1, KCONV):
        pre_act = pre_act + padded[offset:offset + tok_rows] * taps[offset][None, :]
    activated = jax.nn.silu(pre_act).reshape(tok_rows, HEAD_TOTAL, HDIM)
    start_state = jnp.zeros((HEAD_TOTAL, NSTATE, HDIM), jnp.float32)
    scan_out, _ = block_pass(activated, b_float, c_float, logarithm_increments, start_state, min(BLOCK, TOK_DEV))
    ssd_out = (scan_out + head_skip_gain[None, :, None] * activated).reshape(tok_rows, CHANNEL_TOTAL)
    gated_out = ssd_out * jax.nn.silu(gate_float)
    mean_square = lax.optimization_barrier(jnp.mean(gated_out * gated_out, axis=1, keepdims=True))
    return gated_out * lax.rsqrt(mean_square + NORM_EPS) * gated_norm_gain[None, :]

def reference(layer_input_rows, filter_input_channels, gate_input_channels, state_input_vectors, state_output_vectors, decay_logarithm, filter_tap_weight, head_skip_gain, gated_norm_gain, adapter_down_in, adapter_up_in, adapter_down_out, adapter_up_out, output_gradient, base_path_gradient):

    def forward_fn(conv_float, gate_float, b_float, c_float, logarithm_increments):
        return mixer_forward(conv_float, gate_float, b_float, c_float, logarithm_increments, filter_tap_weight, head_skip_gain, gated_norm_gain)
    normed, pullback = jax.vjp(forward_fn, filter_input_channels.astype(jnp.float32), gate_input_channels.astype(jnp.float32), state_input_vectors.astype(jnp.float32), state_output_vectors.astype(jnp.float32), decay_logarithm)
    down_out_factor = adapter_down_out.astype(jnp.float32)
    reverse_out_grad = jnp.dot(output_gradient, adapter_up_out.T, preferred_element_type=jnp.float32)
    normalized_gradient = base_path_gradient.astype(jnp.float32) + ADAPTER_SCALE * jnp.dot(reverse_out_grad, down_out_factor.T, precision=PRECISE_PRODUCT)
    grad_conv, grad_gate, grad_b, grad_c, grad_steps = pullback(normalized_gradient)
    up_in_factor = adapter_up_in.astype(jnp.float32)
    down_in_factor = adapter_down_in.astype(jnp.float32)
    reduced_input = jnp.dot(layer_input_rows, adapter_down_in, preferred_element_type=jnp.float32)
    low_out = jnp.dot(normed, down_out_factor, precision=PRECISE_PRODUCT)
    reverse_in_grad = jnp.dot(grad_conv, up_in_factor[0].T, precision=PRECISE_PRODUCT) + jnp.dot(grad_gate, up_in_factor[1].T, precision=PRECISE_PRODUCT)
    layer_gradient_fn = (ADAPTER_SCALE * jnp.dot(reverse_in_grad, down_in_factor.T, precision=PRECISE_PRODUCT)).astype(jnp.bfloat16)
    averaging_scale = ADAPTER_SCALE / TOKEN_TOTAL
    grad_a_in = averaging_scale * jnp.dot(layer_input_rows.astype(jnp.float32).T, reverse_in_grad, precision=PRECISE_PRODUCT)
    grad_b_in = averaging_scale * jnp.stack([jnp.dot(reduced_input.T, grad_conv, precision=PRECISE_PRODUCT), jnp.dot(reduced_input.T, grad_gate, precision=PRECISE_PRODUCT)])
    grad_a_out = averaging_scale * jnp.dot(normed.T, reverse_out_grad, precision=PRECISE_PRODUCT)
    grad_b_out = averaging_scale * jnp.dot(low_out.T, output_gradient.astype(jnp.float32), precision=PRECISE_PRODUCT)
    return (grad_conv.astype(jnp.bfloat16), grad_gate.astype(jnp.bfloat16), grad_b, grad_c, grad_steps, layer_gradient_fn, grad_a_in, grad_b_in, grad_a_out, grad_b_out)
```

```python
import functools

import jax
import jax.numpy as jnp
from jax import lax
from jax.experimental import pallas as pl
from jax.experimental.pallas import tpu as pltpu
from jax.sharding import PartitionSpec as P

HDIM = 128
NSTATE = 128
BLOCK = 256
SIDE = 8
SLICE = NSTATE // SIDE
MESH = pl.DeviceIdType.MESH
F32 = jnp.float32


PRECISE_PRODUCT = lax.Precision.HIGHEST
ADAPTER_SCALE = 2.0
NORM_EPS = 1e-05


def vmem():
    return pl.BlockSpec(memory_space=pltpu.VMEM)


def along(kind, step):
    if kind == "head":
        place = lax.rem(lax.axis_index("head") + step, SIDE)
        return {"head": place}, place
    seq = lax.axis_index("seq")
    row, col = seq // SIDE, lax.rem(seq, SIDE)
    if kind == "z":
        place = lax.rem(col + step, SIDE)
        return {"seq": row * SIDE + place}, place
    place = lax.rem(row + step, SIDE)
    return {"seq": place * SIDE + col}, place


def own_place(kind):
    if kind == "head":
        return lax.axis_index("head")
    seq = lax.axis_index("seq")
    return lax.rem(seq, SIDE) if kind == "z" else seq // SIDE


def greet(kinds):
    barrier = pltpu.get_barrier_semaphore()
    for kind in kinds:
        for step in range(1, SIDE):
            pl.semaphore_signal(
                barrier, inc=1, device_id=along(kind, step)[0], device_id_type=MESH
            )
    pl.semaphore_wait(barrier, (SIDE - 1) * len(kinds))


def exchange(kind, source, target, send_sem, recv_sem):
    copies = []
    for step in range(1, SIDE):
        device, place = along(kind, step)
        copy = pltpu.make_async_remote_copy(
            src_ref=source(place),
            dst_ref=target,
            send_sem=send_sem.at[step],
            recv_sem=recv_sem.at[step],
            device_id=device,
            device_id_type=MESH,
        )
        copy.start()
        copies.append(copy)
    return copies


def arrived(copies):
    for copy in copies:
        copy.wait_recv()


def left(copies):
    for copy in copies:
        copy.wait_send()


def fold_kernel(
    reverse, own_ref, out_ref, row_in, row_out, part_out, part_in, enter_out, enter_in,
    row_mix, send_sem, recv_sem,
):
    row, col = own_place("y"), own_place("z")
    order = list(range(SIDE))[::-1] if reverse else list(range(SIDE))
    greet(("z", "y"))
    to_owner = exchange(
        "z", lambda place: own_ref.at[place], row_in.at[col], send_sem.at[0], recv_sem.at[0]
    )
    row_in[col] = own_ref[col]
    arrived(to_owner)
    state = jnp.zeros((NSTATE, HDIM), F32)
    total = jnp.zeros((8, HDIM), F32)
    for place in order:
        row_out[place] = state
        row_mix[place] = jnp.exp(total)
        step = row_in[place, NSTATE : NSTATE + 8]
        total = total + step
        state = jnp.exp(step[0:1]) * state + row_in[place, 0:NSTATE]
    for place in range(SIDE):
        part_out[place, 0:SLICE] = state[place * SLICE : (place + 1) * SLICE]
        part_out[place, SLICE : SLICE + 8] = total
    to_part = exchange(
        "y", lambda place: part_out.at[place], part_in.at[row], send_sem.at[1], recv_sem.at[1]
    )
    part_in[row] = part_out[row]
    arrived(to_part)
    part = jnp.zeros((SLICE, HDIM), F32)
    for place in order:
        enter_out[place] = part
        part = jnp.exp(part_in[place, SLICE : SLICE + 1]) * part + part_in[place, 0:SLICE]
    to_row = exchange(
        "y", lambda place: enter_out.at[place], enter_in.at[row], send_sem.at[2], recv_sem.at[2]
    )
    enter_in[row] = enter_out[row]
    arrived(to_row)
    enter = enter_in[...].reshape(NSTATE, HDIM)
    for place in range(SIDE):
        row_out[place] = row_out[place] + row_mix[place, 0:1] * enter
    to_all = exchange(
        "z", lambda place: row_out.at[place], out_ref.at[col], send_sem.at[3], recv_sem.at[3]
    )
    out_ref[col] = row_out[col]
    arrived(to_all)
    for copies in (to_owner, to_part, to_row, to_all):
        left(copies)


def fold(states, total_decay, reverse, collective_id):
    tail = jnp.broadcast_to(total_decay[:, None, None], (SIDE, 8, HDIM))
    return pl.pallas_call(
        functools.partial(fold_kernel, reverse),
        out_shape=jax.ShapeDtypeStruct((SIDE, NSTATE, HDIM), F32),
        in_specs=[vmem()],
        out_specs=vmem(),
        scratch_shapes=[
            pltpu.VMEM((SIDE, NSTATE + 8, HDIM), F32),
            pltpu.VMEM((SIDE, NSTATE, HDIM), F32),
            pltpu.VMEM((SIDE, SLICE + 8, HDIM), F32),
            pltpu.VMEM((SIDE, SLICE + 8, HDIM), F32),
            pltpu.VMEM((SIDE, SLICE, HDIM), F32),
            pltpu.VMEM((SIDE, SLICE, HDIM), F32),
            pltpu.VMEM((SIDE, 8, HDIM), F32),
            pltpu.SemaphoreType.DMA((4, SIDE)),
            pltpu.SemaphoreType.DMA((4, SIDE)),
        ],
        compiler_params=pltpu.CompilerParams(collective_id=collective_id, has_side_effects=True),
    )(jnp.concatenate([states, tail], axis=1))


def head_sum_kernel(own_ref, out_ref, parts, send_sem, recv_sem):
    me = own_place("head")
    greet(("head",))
    copies = exchange("head", lambda place: own_ref, parts.at[me], send_sem, recv_sem)
    parts[me] = own_ref[...]
    arrived(copies)
    total = parts[0]
    for place in range(1, SIDE):
        total = total + parts[place]
    out_ref[...] = total
    left(copies)


def head_sum(x, collective_id):
    return pl.pallas_call(
        head_sum_kernel,
        out_shape=jax.ShapeDtypeStruct(x.shape, F32),
        in_specs=[vmem()],
        out_specs=vmem(),
        scratch_shapes=[
            pltpu.VMEM((SIDE,) + x.shape, F32),
            pltpu.SemaphoreType.DMA((SIDE,)),
            pltpu.SemaphoreType.DMA((SIDE,)),
        ],
        compiler_params=pltpu.CompilerParams(collective_id=collective_id, has_side_effects=True),
    )(x)


def head_scatter_kernel(own_ref, out_ref, parts, send_sem, recv_sem):
    me = own_place("head")
    greet(("head",))
    copies = exchange("head", lambda place: own_ref.at[place], parts.at[me], send_sem, recv_sem)
    parts[me] = own_ref[me]
    arrived(copies)
    total = parts[0]
    for place in range(1, SIDE):
        total = total + parts[place]
    out_ref[...] = total
    left(copies)


def head_scatter(x, collective_id):
    shape = x.shape[1:]
    return pl.pallas_call(
        head_scatter_kernel,
        out_shape=jax.ShapeDtypeStruct(shape, F32),
        in_specs=[vmem()],
        out_specs=vmem(),
        scratch_shapes=[
            pltpu.VMEM((SIDE,) + shape, F32),
            pltpu.SemaphoreType.DMA((SIDE,)),
            pltpu.SemaphoreType.DMA((SIDE,)),
        ],
        compiler_params=pltpu.CompilerParams(collective_id=collective_id, has_side_effects=True),
    )(x)


def token_sum_kernel(own_ref, out_ref, z_in, y_out, y_in, y_sum, z_sum, send_sem, recv_sem):
    row, col = own_place("y"), own_place("z")
    greet(("z", "y"))
    first = exchange(
        "z", lambda place: own_ref.at[place], z_in.at[col], send_sem.at[0], recv_sem.at[0]
    )
    z_in[col] = own_ref[col]
    arrived(first)
    total = z_in[0]
    for place in range(1, SIDE):
        total = total + z_in[place]
    y_out[...] = total
    second = exchange(
        "y", lambda place: y_out.at[place], y_in.at[row], send_sem.at[1], recv_sem.at[1]
    )
    y_in[row] = y_out[row]
    arrived(second)
    total = y_in[0]
    for place in range(1, SIDE):
        total = total + y_in[place]
    y_sum[row] = total
    third = exchange(
        "y", lambda place: y_sum.at[row], y_sum.at[row], send_sem.at[2], recv_sem.at[2]
    )
    arrived(third)
    z_sum[col] = y_sum[...]
    fourth = exchange(
        "z", lambda place: z_sum.at[col], z_sum.at[col], send_sem.at[3], recv_sem.at[3]
    )
    arrived(fourth)
    for copies in (first, second, third, fourth):
        left(copies)
    out_ref[...] = z_sum[...]


def token_sum(x, collective_id):
    line, part = x.shape[1:], x.shape[2:]
    return pl.pallas_call(
        token_sum_kernel,
        out_shape=jax.ShapeDtypeStruct(x.shape, F32),
        in_specs=[vmem()],
        out_specs=vmem(),
        scratch_shapes=[
            pltpu.VMEM((SIDE,) + line, F32),
            pltpu.VMEM(line, F32),
            pltpu.VMEM((SIDE,) + part, F32),
            pltpu.VMEM((SIDE,) + part, F32),
            pltpu.VMEM((SIDE,) + line, F32),
            pltpu.SemaphoreType.DMA((4, SIDE)),
            pltpu.SemaphoreType.DMA((4, SIDE)),
        ],
        compiler_params=pltpu.CompilerParams(collective_id=collective_id, has_side_effects=True),
    )(x)


def running_sum(x):
    rows = x.shape[0]
    lower = (jnp.arange(rows)[:, None] >= jnp.arange(rows)[None, :]).astype(F32)
    return jnp.dot(lower, x, precision=PRECISE_PRODUCT)


def turned_product(x, y):
    return lax.dot_general(y, x, (((0,), (1,)), ((), ())), precision=PRECISE_PRODUCT)


def passed_along(x, axis, by):
    devices = lax.axis_size(axis)
    pairs = [(i, i + by) for i in range(devices) if 0 <= i + by < devices]
    return lax.ppermute(x, axis, pairs)


def block_pass(activated, b_float, c_float, logarithm_increments, start_state, block_rows):
    tok_rows, head_count, head_width = activated.shape
    block_count = tok_rows // block_rows
    state_width = b_float.shape[1]
    causal = (jnp.arange(block_rows)[:, None] >= jnp.arange(block_rows)[None, :])[None, :, :]

    def advance(carried_state, block_items):
        x_block, b_block, c_block, l_block = block_items
        cum_decay = running_sum(l_block)
        cum_heads = cum_decay.T
        decay_gap = jnp.where(causal, cum_heads[:, :, None] - cum_heads[:, None, :], 0.0)
        decays = jnp.where(causal, jnp.exp(decay_gap), 0.0)
        scores = jnp.dot(c_block, b_block.T, precision=PRECISE_PRODUCT)
        weights = decays * scores[None, :, :]
        inner_out = jnp.einsum("hts,shp->thp", weights, x_block, precision=PRECISE_PRODUCT)
        outer_out = jnp.exp(cum_decay)[:, :, None] * jnp.einsum(
            "tn,hnp->thp", c_block, carried_state, precision=PRECISE_PRODUCT
        )
        to_end = jnp.exp(cum_decay[-1][None, :] - cum_decay)
        fresh_state = jnp.einsum(
            "sn,shp->hnp", b_block, x_block * to_end[:, :, None], precision=PRECISE_PRODUCT
        )
        next_state = jnp.exp(cum_decay[-1])[:, None, None] * carried_state + fresh_state
        return (next_state, inner_out + outer_out)

    block_items = (
        activated.reshape(block_count, block_rows, head_count, head_width),
        b_float.reshape(block_count, block_rows, state_width),
        c_float.reshape(block_count, block_rows, state_width),
        logarithm_increments.reshape(block_count, block_rows, head_count),
    )
    end_state, outputs = lax.scan(advance, start_state, block_items)
    return (outputs.reshape(tok_rows, head_count, head_width), end_state)


def carried(c_float, logarithm_increments, state_in):
    cum_decay = running_sum(logarithm_increments)
    outer_out = jnp.exp(cum_decay)[:, :, None] * jnp.einsum(
        "tn,hnp->thp", c_float, state_in, precision=PRECISE_PRODUCT
    )
    passed = jnp.exp(cum_decay[-1])[:, None, None] * state_in
    return (outer_out, passed)


def end_state(activated, b_float, logarithm_increments):
    cum_decay = running_sum(logarithm_increments)
    to_end = jnp.exp(cum_decay[-1][None, :] - cum_decay)
    return jnp.einsum(
        "sn,shp->hnp", b_float, activated * to_end[:, :, None], precision=PRECISE_PRODUCT
    )


def body(
    layer_input_rows,
    filter_input_channels,
    gate_input_channels,
    state_input_vectors,
    state_output_vectors,
    decay_logarithm,
    filter_tap_weight,
    head_skip_gain,
    gated_norm_gain,
    adapter_down_in,
    adapter_up_in,
    adapter_down_out,
    adapter_up_out,
    output_gradient,
    base_path_gradient,
):
    tok_rows, chan_width = filter_input_channels.shape
    head_count = decay_logarithm.shape[1]
    rim_rows = filter_tap_weight.shape[0] - 1
    block_rows = min(BLOCK, tok_rows)
    row_total_count = tok_rows * lax.axis_size("seq")
    all_channels = chan_width * lax.axis_size("head")
    taps = filter_tap_weight.astype(jnp.float32)
    before = passed_along(filter_input_channels[tok_rows - rim_rows :], "seq", 1)
    padded = jnp.concatenate([before, filter_input_channels], axis=0).astype(jnp.float32)
    pre_act = padded[0:tok_rows] * taps[0][None, :]
    for offset in range(1, rim_rows + 1):
        pre_act = pre_act + padded[offset : offset + tok_rows] * taps[offset][None, :]
    act_heads = jax.nn.silu(pre_act).reshape(tok_rows, head_count, HDIM)
    b_float = state_input_vectors.astype(jnp.float32)
    c_float = state_output_vectors.astype(jnp.float32)
    zero_state = jnp.zeros((head_count, NSTATE, HDIM), jnp.float32)

    def local_pass(activated, b_part, c_part, logarithm_increments):
        return block_pass(activated, b_part, c_part, logarithm_increments, zero_state, block_rows)

    (inner_out, fresh_state), pull_local = jax.vjp(
        local_pass, act_heads, b_float, c_float, decay_logarithm
    )
    total_decay = jnp.sum(decay_logarithm, axis=0)
    state_in = fold(fresh_state, total_decay, False, 0)
    (outer_out, _), pull_carry = jax.vjp(carried, c_float, decay_logarithm, state_in)
    ssd_out = inner_out + outer_out + head_skip_gain[None, :, None] * act_heads
    mixer_out = ssd_out.reshape(tok_rows, chan_width)
    gate_float = gate_input_channels.astype(jnp.float32)
    gate_sig = jax.nn.sigmoid(gate_float)
    gated_out = mixer_out * gate_float * gate_sig
    square_part = jnp.sum(gated_out * gated_out, axis=1)
    scaled = gated_out * gated_norm_gain[None, :]
    down_out_factor = adapter_down_out.astype(jnp.float32)
    early = head_sum(
        jnp.concatenate(
            [
                lax.dot_general(
                    adapter_up_out,
                    output_gradient,
                    (((1,), (1,)), ((), ())),
                    preferred_element_type=jnp.float32,
                ),
                lax.dot_general(
                    adapter_down_in,
                    layer_input_rows,
                    (((0,), (1,)), ((), ())),
                    preferred_element_type=jnp.float32,
                ),
            ],
            axis=0,
        ),
        1,
    )
    rank = adapter_up_out.shape[0]
    reverse_out_grad = early[:rank].T
    reduced_input = early[rank:].T
    normalized_gradient = base_path_gradient.astype(jnp.float32) + ADAPTER_SCALE * jnp.dot(
        reverse_out_grad, down_out_factor.T, precision=PRECISE_PRODUCT
    )
    weighted = normalized_gradient * gated_norm_gain[None, :]
    late = head_sum(
        jnp.concatenate(
            [
                turned_product(scaled, down_out_factor),
                square_part[None, :],
                jnp.sum(weighted * gated_out, axis=1)[None, :],
                jnp.zeros((6, tok_rows), jnp.float32),
            ],
            axis=0,
        ),
        2,
    )
    inv_rms = lax.rsqrt(late[rank] / all_channels + NORM_EPS)
    normed = scaled * inv_rms[:, None]
    low_out = late[:rank].T * inv_rms[:, None]
    dot_total = late[rank + 1]
    grad_gated = (
        inv_rms[:, None] * weighted
        - gated_out * (inv_rms * inv_rms * inv_rms * dot_total / all_channels)[:, None]
    )
    grad_mixer = grad_gated * gate_float * gate_sig
    grad_gate = grad_gated * mixer_out * gate_sig * (1.0 + gate_float * (1.0 - gate_sig))
    grad_ssd = grad_mixer.reshape(tok_rows, head_count, HDIM)
    cum_decay = running_sum(decay_logarithm)
    local_grad = jnp.einsum(
        "tn,thp->hnp", c_float, grad_ssd * jnp.exp(cum_decay)[:, :, None], precision=PRECISE_PRODUCT
    )
    state_grad = fold(local_grad, total_decay, True, 3)
    grad_act, grad_b, grad_c, grad_steps = pull_local((grad_ssd, state_grad))
    carry_c, carry_steps, _ = pull_carry((grad_ssd, state_grad))
    grad_c = grad_c + carry_c
    grad_steps = grad_steps + carry_steps
    grad_act = grad_act + head_skip_gain[None, :, None] * grad_ssd
    pre_sig = jax.nn.sigmoid(pre_act)
    grad_pre = grad_act.reshape(tok_rows, chan_width) * pre_sig * (1.0 + pre_act * (1.0 - pre_sig))
    after = passed_along(grad_pre[:rim_rows], "seq", -1)
    extended = jnp.concatenate([grad_pre, after], axis=0)
    grad_conv = extended[rim_rows : rim_rows + tok_rows] * taps[0][None, :]
    for offset in range(1, rim_rows + 1):
        grad_conv = (
            grad_conv
            + extended[rim_rows - offset : rim_rows - offset + tok_rows] * taps[offset][None, :]
        )
    own_rows = tok_rows // SIDE
    grad_rows = head_scatter(
        jnp.concatenate(
            [grad_b.reshape(SIDE, own_rows, NSTATE), grad_c.reshape(SIDE, own_rows, NSTATE)], axis=1
        ),
        4,
    )
    grad_b_rows, grad_c_rows = grad_rows[:own_rows], grad_rows[own_rows:]
    up_in_factor = adapter_up_in.astype(jnp.float32)
    back_part = turned_product(grad_conv, up_in_factor[0].T) + turned_product(
        grad_gate, up_in_factor[1].T
    )
    reverse_in_grad = head_sum(back_part, 5).T
    layer_gradient_fn = (
        ADAPTER_SCALE
        * jnp.dot(reverse_in_grad, adapter_down_in.astype(jnp.float32).T, precision=PRECISE_PRODUCT)
    ).astype(jnp.bfloat16)
    averaging_scale = ADAPTER_SCALE / row_total_count
    wide = jnp.concatenate(
        [
            turned_product(layer_input_rows.astype(jnp.float32).T, reverse_in_grad),
            jnp.dot(reduced_input.T, grad_conv, precision=PRECISE_PRODUCT),
            jnp.dot(reduced_input.T, grad_gate, precision=PRECISE_PRODUCT),
            turned_product(normed.T, reverse_out_grad),
            jnp.dot(low_out.T, output_gradient.astype(jnp.float32), precision=PRECISE_PRODUCT),
        ],
        axis=1,
    )
    lanes = wide.shape[1] // SIDE // SIDE
    pieces = averaging_scale * wide.reshape(rank, SIDE * SIDE, lanes)
    pieces = pieces.transpose(1, 0, 2).reshape(SIDE, SIDE, rank * lanes // 128, 128)
    summed = token_sum(pieces, 6).reshape(SIDE * SIDE, rank, lanes)
    summed = summed.transpose(1, 0, 2).reshape(rank, wide.shape[1])
    width = layer_input_rows.shape[1]
    grad_a_in = summed[:, :width].T
    grad_b_in = jnp.stack(
        [
            summed[:, width : width + chan_width],
            summed[:, width + chan_width : width + 2 * chan_width],
        ]
    )
    grad_a_out = summed[:, width + 2 * chan_width : width + 3 * chan_width].T
    grad_b_out = summed[:, width + 3 * chan_width :]
    return (
        grad_conv.astype(jnp.bfloat16),
        grad_gate.astype(jnp.bfloat16),
        grad_b_rows,
        grad_c_rows,
        grad_steps,
        layer_gradient_fn,
        grad_a_in,
        grad_b_in,
        grad_a_out,
        grad_b_out,
    )


def solution(mesh):
    in_specs = (
        P("seq", "head"),
        P("seq", "head"),
        P("seq", "head"),
        P("seq", None),
        P("seq", None),
        P("seq", "head"),
        P(None, "head"),
        P("head"),
        P("head"),
        P("head", None),
        P(None, None, "head"),
        P("head", None),
        P(None, "head"),
        P("seq", "head"),
        P("seq", "head"),
    )
    out_specs = (
        P("seq", "head"),
        P("seq", "head"),
        P(("seq", "head"), None),
        P(("seq", "head"), None),
        P("seq", "head"),
        P("seq", "head"),
        P("head", None),
        P(None, None, "head"),
        P("head", None),
        P(None, "head"),
    )
    return jax.shard_map(body, mesh=mesh, in_specs=in_specs, out_specs=out_specs, check_vma=False)
```

```python
import jax
import jax.numpy as jnp
from jax import lax
from jax.experimental import pallas as pl
from jax.experimental.pallas import tpu as pltpu
from jax.sharding import PartitionSpec as P

ADAPTER_SCALE = 2.0
NORM_EPS = 1e-05
SIDE = 8
HDIM = 128
NSTATE = 128
TOK = 128
RANK = 32
KCONV = 4
SLICE = NSTATE // SIDE
OWN = TOK // SIDE
EARLY = 80
LATE = 48
MESH = pl.DeviceIdType.MESH
F32 = jnp.float32
BF16 = jnp.bfloat16


def own_place(kind):
    if kind == "head":
        return lax.axis_index("head")
    seq = lax.axis_index("seq")
    return lax.rem(seq, SIDE) if kind == "z" else seq // SIDE


def along(kind, step):
    if kind == "head":
        place = lax.rem(lax.axis_index("head") + step, SIDE)
        return {"head": place}, place
    seq = lax.axis_index("seq")
    if kind == "seq":
        place = lax.rem(seq + step + SIDE * SIDE, SIDE * SIDE)
        return {"seq": place}, place
    row, col = seq // SIDE, lax.rem(seq, SIDE)
    if kind == "z":
        place = lax.rem(col + step, SIDE)
        return {"seq": row * SIDE + place}, place
    place = lax.rem(row + step, SIDE)
    return {"seq": place * SIDE + col}, place


def send(device, source, target, send_sem, recv_sem):
    copy = pltpu.make_async_remote_copy(
        src_ref=source,
        dst_ref=target,
        send_sem=send_sem,
        recv_sem=recv_sem,
        device_id=device,
        device_id_type=MESH,
    )
    copy.start()
    return copy


class Copies:
    def __init__(self, send_sem, recv_sem):
        self.send_sem, self.recv_sem, self.used, self.all = send_sem, recv_sem, 0, []

    def start(self, device, source, target):
        at = self.used
        self.used += 1
        copy = send(device, source, target, self.send_sem.at[at], self.recv_sem.at[at])
        self.all.append(copy)
        return copy

    def exchange(self, kind, source, target):
        started = []
        for step in range(1, SIDE):
            device, place = along(kind, step)
            started.append(self.start(device, source(place), target))
        return started

    def left(self):
        for copy in self.all:
            copy.wait_send()


def arrived(copies):
    for copy in copies:
        copy.wait_recv()


def nn(a, b):
    return lax.dot_general(a, b, (((1,), (0,)), ((), ())), preferred_element_type=F32)


def nt(a, b):
    return lax.dot_general(a, b, (((1,), (1,)), ((), ())), preferred_element_type=F32)


def split(x):
    high = x.astype(BF16)
    return high, (x - high.astype(F32)).astype(BF16)


def left_exact(a, x, product=nn):
    high, low = split(x)
    return product(a, high) + product(a, low)


def right_exact(x, a, product=nn):
    high, low = split(x)
    return product(high, a) + product(low, a)


def both(x, y, product=nn):
    xh, xl = split(x)
    yh, yl = split(y)
    return product(xh, yh) + (product(xh, yl) + product(xl, yh))


def precise(a, b):
    return lax.dot_general(
        a, b, (((1,), (0,)), ((), ())), precision=lax.Precision.HIGHEST, preferred_element_type=F32
    )


def turned(x):
    missing = 128 - x.shape[1]
    if missing:
        x = jnp.concatenate([x, jnp.zeros((x.shape[0], missing), F32)], axis=1)
    return x.T


def sigmoid(x):
    return 1.0 / (1.0 + jnp.exp(-x))


def lanes(h):
    return pl.ds(pl.multiple_of(h * HDIM, HDIM), HDIM)


def each_head(step):
    lax.fori_loop(0, SIDE, lambda h, c: (step(h), c)[1], 0)


class Fold:
    def __init__(self, copies, refs, reverse):
        self.copies = copies
        (
            self.own, self.row_in, self.row_out, self.row_mix, self.part_out, self.part_in,
            self.enter_out, self.enter_in, self.out,
        ) = refs
        self.order = list(range(SIDE))[::-1] if reverse else list(range(SIDE))
        self.row, self.col = own_place("y"), own_place("z")

    def to_owner(self):
        self.flight = self.copies.exchange(
            "z", lambda place: self.own.at[place], self.row_in.at[self.col]
        )
        self.row_in[self.col] = self.own[self.col]

    def to_part(self):
        arrived(self.flight)
        state = jnp.zeros((NSTATE, HDIM), F32)
        total = jnp.zeros((8, HDIM), F32)
        for place in self.order:
            self.row_out[place] = state
            self.row_mix[place] = jnp.exp(total)
            step = self.row_in[place, NSTATE : NSTATE + 8]
            total = total + step
            state = jnp.exp(step[0:1]) * state + self.row_in[place, 0:NSTATE]
        for place in range(SIDE):
            self.part_out[place, 0:SLICE] = state[place * SLICE : (place + 1) * SLICE]
            self.part_out[place, SLICE : SLICE + 8] = total
        self.flight = self.copies.exchange(
            "y", lambda place: self.part_out.at[place], self.part_in.at[self.row]
        )
        self.part_in[self.row] = self.part_out[self.row]

    def to_row(self):
        arrived(self.flight)
        part = jnp.zeros((SLICE, HDIM), F32)
        for place in self.order:
            self.enter_out[place] = part
            decay = jnp.exp(self.part_in[place, SLICE : SLICE + 1])
            part = decay * part + self.part_in[place, 0:SLICE]
        self.flight = self.copies.exchange(
            "y", lambda place: self.enter_out.at[place], self.enter_in.at[self.row]
        )
        self.enter_in[self.row] = self.enter_out[self.row]

    def to_all(self):
        arrived(self.flight)
        enter = self.enter_in[...].reshape(NSTATE, HDIM)
        for place in range(SIDE):
            self.row_out[place] = self.row_out[place] + self.row_mix[place, 0:1] * enter
        self.flight = self.copies.exchange(
            "z", lambda place: self.row_out.at[place], self.out.at[self.col]
        )
        self.out[self.col] = self.row_out[self.col]

    def end(self):
        arrived(self.flight)


def fold_scratch():
    return [
        pltpu.VMEM((SIDE, NSTATE + 8, HDIM), F32),
        pltpu.VMEM((SIDE, NSTATE + 8, HDIM), F32),
        pltpu.VMEM((SIDE, NSTATE, HDIM), F32),
        pltpu.VMEM((SIDE, 8, HDIM), F32),
        pltpu.VMEM((SIDE, SLICE + 8, HDIM), F32),
        pltpu.VMEM((SIDE, SLICE + 8, HDIM), F32),
        pltpu.VMEM((SIDE, SLICE, HDIM), F32),
        pltpu.VMEM((SIDE, SLICE, HDIM), F32),
        pltpu.VMEM((SIDE, NSTATE, HDIM), F32),
    ]


class TokenSum:
    def __init__(self, copies, refs):
        self.copies = copies
        self.own, self.z_in, self.y_out, self.y_in, self.all = refs
        self.row, self.col = own_place("y"), own_place("z")

    def to_owner(self):
        self.flight = self.copies.exchange(
            "z", lambda place: self.own.at[place], self.z_in.at[self.col]
        )
        self.z_in[self.col] = self.own[self.col]

    def total(self, ref):
        total = ref[0]
        for place in range(1, SIDE):
            total = total + ref[place]
        return total

    def to_row(self):
        arrived(self.flight)
        self.y_out[...] = self.total(self.z_in)
        self.flight = self.copies.exchange("y", lambda place: self.y_out, self.y_in.at[self.row])
        self.y_in[self.row] = self.y_out[...]

    def to_all(self):
        arrived(self.flight)
        self.all[self.col] = self.total(self.y_in)
        self.flight = self.copies.exchange(
            "z", lambda place: self.all.at[self.col], self.all.at[self.col]
        )

    def end(self):
        arrived(self.flight)


def token_sum_scratch(rows):
    return [
        pltpu.VMEM((SIDE, rows, HDIM), F32),
        pltpu.VMEM((SIDE, rows, HDIM), F32),
        pltpu.VMEM((rows, HDIM), F32),
        pltpu.VMEM((SIDE, rows, HDIM), F32),
        pltpu.VMEM((SIDE, rows, HDIM), F32),
    ]


def head_total(ref):
    total = ref[0]
    for place in range(1, SIDE):
        total = total + ref[place]
    return total


COPIES = 2 + 4 * 7 + 2 * 4 * 7 + 2 * 3 * 7
WIDE = 13


def kernel(
    x_ref, conv_ref, gate_ref, b_ref, c_ref, l_ref, tap_ref, skip_ref, gain_ref, down_in_ref,
    up_in_ref, down_out_ref, up_out_ref, og_ref, base_ref,
    gconv_ref, ggate_ref, gb_ref, gc_ref, gl_ref, glayer_ref, ga_in_ref, gb_in_ref, ga_out_ref,
    gb_out_ref,
    *scratch,
):
    scratch = list(scratch)

    def take(n):
        out = scratch[:n]
        del scratch[:n]
        return out

    fold_refs, back_refs = take(9), take(9)
    early_refs, late_refs = take(5), take(5)
    (
        pre3, act3, slope3, y3, outer3, mix3, decay3, weighted3, gs3, dgs3, gssd3, ecum3, toend3,
    ) = take(WIDE)
    (cum_row, ext, halo, gext, halo_g, first_own, first_all, mid_own, mid_all, low_own, low_all,
     bc_own, bc_all, dcum3, gc_acc, gb_acc, dg_acc) = take(17)
    send_sem, recv_sem = take(2)

    seq, head = lax.axis_index("seq"), lax.axis_index("head")
    copies = Copies(send_sem, recv_sem)
    barrier = pltpu.get_barrier_semaphore()
    greeted = 0
    for kind, steps in (
        ("z", range(1, SIDE)), ("y", range(1, SIDE)), ("head", range(1, SIDE)), ("seq", (1, -1))
    ):
        for step in steps:
            pl.semaphore_signal(
                barrier, inc=1, device_id=along(kind, step)[0], device_id_type=MESH
            )
            greeted += 1

    first_own[0:RANK] = nt(up_out_ref[...], og_ref[...])
    first_own[RANK : 2 * RANK] = turned(nn(x_ref[...], down_in_ref[...]))[0:RANK]
    pl.semaphore_wait(barrier, greeted)
    tail = copies.start(along("seq", 1)[0], conv_ref.at[TOK - 16 : TOK], halo)
    first = copies.exchange("head", lambda place: first_own, first_all.at[head])
    first_all[head] = first_own[...]

    rows_at = lax.broadcasted_iota(jnp.int32, (TOK, TOK), 0)
    cols_at = lax.broadcasted_iota(jnp.int32, (TOK, TOK), 1)
    causal = rows_at >= cols_at
    cum = precise(causal.astype(F32), l_ref[...])
    cum_turned = turned(cum)[0:SIDE]
    cum_row[...] = cum_turned
    for h in range(SIDE):
        col = jnp.broadcast_to(cum[:, h : h + 1], (TOK, TOK))
        last = cum[TOK - 1 : TOK, h : h + 1]
        gap = col - cum_turned[h : h + 1]
        decay3[h] = jnp.where(causal, jnp.exp(jnp.where(causal, gap, 0.0)), 0.0)
        ecum3[h] = jnp.exp(col)
        toend3[h] = jnp.exp(jnp.broadcast_to(last, (TOK, TOK)) - col)
        total = jnp.broadcast_to(last, (8, HDIM))
        fold_refs[0][h, NSTATE : NSTATE + 8] = total
        back_refs[0][h, NSTATE : NSTATE + 8] = total
    b_turned = b_ref[...].astype(F32).T.astype(BF16)
    c_turned = c_ref[...].astype(F32).T.astype(BF16)
    scores = nt(c_ref[...], b_ref[...])
    scores_turned = nt(b_ref[...], c_ref[...])

    ext[8 : TOK + 8] = conv_ref[...].astype(F32)
    tail.wait_recv()
    before = halo[...].astype(F32)[8:16]
    ext[0:8] = jnp.where(seq > 0, before, 0.0)

    def local_state(h):
        at = lanes(h)
        taps = tap_ref[:, at].astype(F32)
        pre = ext[5 : 5 + TOK, at] * taps[0:1]
        for k in range(1, KCONV):
            pre = pre + ext[5 + k : 5 + k + TOK, at] * taps[k : k + 1]
        sig = sigmoid(pre)
        act = pre * sig
        act3[h] = act
        slope3[h] = sig * (1.0 + pre * (1.0 - sig))
        fold_refs[0][h, 0:NSTATE] = left_exact(b_turned, act * toend3[h])

    each_head(local_state)
    fold = Fold(copies, fold_refs, False)
    fold.to_owner()

    def inner(h):
        mix = decay3[h] * scores
        y3[h] = both(mix, act3[h]) + skip_ref[h] * act3[h]

    each_head(inner)
    fold.to_part()

    arrived(first)
    sums = head_total(first_all)
    back_out_turned = sums[0:RANK]
    low_in_turned = sums[RANK : 2 * RANK]
    back_out = turned(jnp.concatenate([back_out_turned, jnp.zeros((96, TOK), F32)], axis=0))[:, 0:RANK]

    def norm_gradient(h):
        at = lanes(h)
        down = down_out_ref[pl.ds(pl.multiple_of(h * HDIM, HDIM), HDIM), :]
        weighted3[h] = (
            base_ref[:, at].astype(F32) + ADAPTER_SCALE * right_exact(back_out, down, nt)
        ) * gain_ref[:, at]
        gate = gate_ref[:, at].astype(F32)
        sig = sigmoid(gate)
        gs3[h] = gate * sig
        dgs3[h] = sig * (1.0 + gate * (1.0 - sig))

    each_head(norm_gradient)
    fold.to_row()
    fold.to_all()
    fold.end()
    state_in = fold.out

    def gated_sums(h, carry):
        square, dot, low = carry
        at = lanes(h)
        outer = ecum3[h] * left_exact(c_ref[...], state_in[h])
        outer3[h] = outer
        y = y3[h] + outer
        y3[h] = y
        gated = y * gs3[h]
        down = down_out_ref[pl.ds(pl.multiple_of(h * HDIM, HDIM), HDIM), :]
        square = square + gated * gated
        dot = dot + weighted3[h] * gated
        low = low + right_exact(gated * gain_ref[:, at], down)
        return square, dot, low

    square, dot, low = lax.fori_loop(
        0, SIDE, gated_sums,
        (jnp.zeros((TOK, HDIM), F32), jnp.zeros((TOK, HDIM), F32), jnp.zeros((TOK, RANK), F32)),
    )
    mid_own[...] = turned(
        jnp.concatenate(
            [
                low,
                jnp.sum(square, axis=1, keepdims=True),
                jnp.sum(dot, axis=1, keepdims=True),
                jnp.zeros((TOK, 128 - RANK - 2), F32),
            ],
            axis=1,
        )
    )[0 : RANK + 8]
    mid = copies.exchange("head", lambda place: mid_own, mid_all.at[head])
    mid_all[head] = mid_own[...]
    arrived(mid)
    sums = head_total(mid_all)
    inv_row = lax.rsqrt(sums[RANK : RANK + 1] / (SIDE * SIDE * HDIM) + NORM_EPS)
    kappa_row = inv_row * inv_row * inv_row * sums[RANK + 1 : RANK + 2] / (SIDE * SIDE * HDIM)
    low_out_turned = sums[0:RANK] * inv_row
    columns = turned(jnp.concatenate([inv_row, kappa_row, jnp.zeros((126, TOK), F32)], axis=0))
    inv = jnp.broadcast_to(columns[:, 0:1], (TOK, HDIM))
    kappa = jnp.broadcast_to(columns[:, 1:2], (TOK, HDIM))

    def mixer_gradient(h):
        gated = y3[h] * gs3[h]
        grad_gated = inv * weighted3[h] - gated * kappa
        gssd = grad_gated * gs3[h]
        gssd3[h] = gssd
        pre3[h] = grad_gated * y3[h] * dgs3[h]
        back_refs[0][h, 0:NSTATE] = left_exact(c_turned, gssd * ecum3[h])

    each_head(mixer_gradient)
    back = Fold(copies, back_refs, True)
    back.to_owner()

    gc_acc[...] = jnp.zeros((TOK, NSTATE), F32)
    dg_acc[...] = jnp.zeros((TOK, TOK), F32)

    def local_gradient(h):
        gssd = gssd3[h]
        act = act3[h]
        decay = decay3[h]
        part = both(gssd, act, nt) * decay
        dg_acc[...] += part
        moved = part * scores
        away = turned(moved)
        dcum3[h] = moved - away + gssd * outer3[h]
        mix_turned = turned(decay) * scores_turned
        mix3[h] = both(mix_turned, gssd) + skip_ref[h] * gssd
        gc_acc[...] += both(gssd * ecum3[h], state_in[h], nt)

    each_head(local_gradient)
    back.to_part()

    scale = ADAPTER_SCALE / (SIDE * SIDE * TOK)
    early = TokenSum(copies, early_refs)

    def early_parts(h):
        at = lanes(h)
        ggate = pre3[h]
        ggate_ref[:, at] = ggate.astype(BF16)
        early.own[h, 0:RANK] = scale * both(low_in_turned, ggate)
        normed = y3[h] * gs3[h] * gain_ref[:, at] * inv
        early.own[h, RANK : 2 * RANK] = scale * both(back_out_turned, normed)

    each_head(early_parts)
    back.to_row()
    dg = dg_acc[...]
    gc_acc[...] += right_exact(dg, b_ref[...])
    gb_acc[...] = right_exact(turned(dg), c_ref[...])
    grad_b_out = scale * right_exact(low_out_turned, og_ref[...])
    for part in range(SIDE):
        early.own[part, 2 * RANK : 2 * RANK + 16] = grad_b_out[
            16 * (part % 2) : 16 * (part % 2) + 16, HDIM * (part // 2) : HDIM * (part // 2 + 1)
        ]
    back.to_all()
    early.to_owner()
    back.end()
    state_grad = back.out

    def state_gradient(h):
        toend = toend3[h]
        act = act3[h]
        into = toend * left_exact(b_ref[...], state_grad[h])
        gb_acc[...] += both(act * toend, state_grad[h], nt)
        fell = act * into
        total = jnp.sum(fell, axis=0, keepdims=True) + ecum3[h, TOK - 1 : TOK] * jnp.sum(
            state_in[h] * state_grad[h], axis=0, keepdims=True
        )
        dcum = dcum3[h] - fell
        dcum3[h] = jnp.where(rows_at == TOK - 1, dcum + total, dcum)
        gpre = (mix3[h] + into) * slope3[h]
        gext[0:TOK, lanes(h)] = gpre

    each_head(state_gradient)
    rim = copies.start(along("seq", -1)[0], gext.at[0:8], halo_g)
    for part in range(SIDE):
        bc_own[part, 0:OWN] = gb_acc[OWN * part : OWN * (part + 1)]
        bc_own[part, OWN : 2 * OWN] = gc_acc[OWN * part : OWN * (part + 1)]
    rows_out = copies.exchange("head", lambda place: bc_own.at[place], bc_all.at[head])
    bc_all[head] = bc_own[head]
    early.to_row()
    dcum = jnp.concatenate(
        [jnp.sum(dcum3[h], axis=1, keepdims=True) for h in range(SIDE)], axis=1
    )
    gl_ref[...] = precise((rows_at <= cols_at).astype(F32), dcum)
    rim.wait_recv()
    gext[TOK : TOK + 8] = jnp.where(seq < SIDE * SIDE - 1, halo_g[...], 0.0)
    late = TokenSum(copies, late_refs)

    def conv_gradient(h, low):
        at = lanes(h)
        taps = tap_ref[:, at].astype(F32)
        gconv = gext[3 : 3 + TOK, at] * taps[0:1]
        for k in range(1, KCONV):
            gconv = gconv + gext[3 - k : 3 - k + TOK, at] * taps[k : k + 1]
        gconv_ref[:, at] = gconv.astype(BF16)
        late.own[h, 0:RANK] = scale * both(low_in_turned, gconv)
        return low + (
            left_exact(up_in_ref[0, :, at], gconv, nt) + left_exact(up_in_ref[1, :, at], pre3[h], nt)
        )

    low_own[...] = lax.fori_loop(0, SIDE, conv_gradient, jnp.zeros((RANK, TOK), F32))
    low = copies.exchange("head", lambda place: low_own, low_all.at[head])
    low_all[head] = low_own[...]
    early.to_all()
    arrived(low)
    back_in_turned = head_total(low_all)
    grad_a_in = scale * right_exact(back_in_turned, x_ref[...])
    for part in range(SIDE):
        late.own[part, RANK : RANK + 16] = grad_a_in[
            16 * (part % 2) : 16 * (part % 2) + 16, HDIM * (part // 2) : HDIM * (part // 2 + 1)
        ]
    late.to_owner()
    back_in = turned(jnp.concatenate([back_in_turned, jnp.zeros((96, TOK), F32)], axis=0))[:, 0:RANK]
    glayer_ref[...] = (ADAPTER_SCALE * right_exact(back_in, down_in_ref[...], nt)).astype(BF16)
    arrived(rows_out)
    sums = head_total(bc_all)
    gb_ref[...] = sums[0:OWN]
    gc_ref[...] = sums[OWN : 2 * OWN]
    late.to_row()
    early.end()
    pad = jnp.zeros((96, HDIM), F32)
    for part in range(SIDE):
        at = slice(HDIM * part, HDIM * (part + 1))
        gb_in_ref[1, :, at] = early.all[part, 0:RANK]
        ga_out_ref[at, :] = turned(
            jnp.concatenate([early.all[part, RANK : 2 * RANK], pad], axis=0)
        )[:, 0:RANK]
        gb_out_ref[
            16 * (part % 2) : 16 * (part % 2) + 16, HDIM * (part // 2) : HDIM * (part // 2 + 1)
        ] = early.all[part, 2 * RANK : 2 * RANK + 16]
    late.to_all()
    late.end()
    for part in range(SIDE):
        gb_in_ref[0, :, HDIM * part : HDIM * (part + 1)] = late.all[part, 0:RANK]
    for part in range(SIDE // 2):
        ga_in_ref[HDIM * part : HDIM * (part + 1), :] = turned(
            jnp.concatenate(
                [
                    late.all[2 * part, RANK : RANK + 16],
                    late.all[2 * part + 1, RANK : RANK + 16],
                    pad,
                ],
                axis=0,
            )
        )[:, 0:RANK]
    copies.left()


def body(x, conv, gate, b, c, l, taps, skip, gain, down_in, up_in, down_out, up_out, og, base):
    outs = [
        jax.ShapeDtypeStruct(conv.shape, BF16),
        jax.ShapeDtypeStruct(gate.shape, BF16),
        jax.ShapeDtypeStruct((OWN, NSTATE), F32),
        jax.ShapeDtypeStruct((OWN, NSTATE), F32),
        jax.ShapeDtypeStruct(l.shape, F32),
        jax.ShapeDtypeStruct(x.shape, BF16),
        jax.ShapeDtypeStruct(down_in.shape, F32),
        jax.ShapeDtypeStruct(up_in.shape, F32),
        jax.ShapeDtypeStruct(down_out.shape, F32),
        jax.ShapeDtypeStruct(up_out.shape, F32),
    ]
    specs = [pl.BlockSpec(memory_space=pltpu.VMEM) for _ in range(15)]
    specs[7] = pl.BlockSpec(memory_space=pltpu.SMEM)
    wide = conv.shape[1]
    results = pl.pallas_call(
        kernel,
        out_shape=outs,
        in_specs=specs,
        out_specs=[pl.BlockSpec(memory_space=pltpu.VMEM) for _ in outs],
        scratch_shapes=fold_scratch()
        + fold_scratch()
        + token_sum_scratch(EARLY)
        + token_sum_scratch(LATE)
        + [pltpu.VMEM((SIDE, TOK, HDIM), F32) for _ in range(WIDE)]
        + [
            pltpu.VMEM((SIDE, TOK), F32),
            pltpu.VMEM((TOK + 8, wide), F32),
            pltpu.VMEM((16, wide), BF16),
            pltpu.VMEM((TOK + 8, wide), F32),
            pltpu.VMEM((8, wide), F32),
            pltpu.VMEM((2 * RANK, TOK), F32),
            pltpu.VMEM((SIDE, 2 * RANK, TOK), F32),
            pltpu.VMEM((RANK + 8, TOK), F32),
            pltpu.VMEM((SIDE, RANK + 8, TOK), F32),
            pltpu.VMEM((RANK, TOK), F32),
            pltpu.VMEM((SIDE, RANK, TOK), F32),
            pltpu.VMEM((SIDE, 2 * OWN, NSTATE), F32),
            pltpu.VMEM((SIDE, 2 * OWN, NSTATE), F32),
            pltpu.VMEM((SIDE, TOK, HDIM), F32),
            pltpu.VMEM((TOK, NSTATE), F32),
            pltpu.VMEM((TOK, NSTATE), F32),
            pltpu.VMEM((TOK, TOK), F32),
            pltpu.SemaphoreType.DMA((COPIES,)),
            pltpu.SemaphoreType.DMA((COPIES,)),
        ],
        compiler_params=pltpu.CompilerParams(
            collective_id=0, has_side_effects=True, vmem_limit_bytes=48 << 20
        ),
    )(
        x, conv, gate, b, c, l, taps, skip, gain.reshape(1, wide), down_in, up_in, down_out,
        up_out, og, base,
    )
    return tuple(results)


def solution(mesh):
    in_specs = (
        P("seq", "head"),
        P("seq", "head"),
        P("seq", "head"),
        P("seq", None),
        P("seq", None),
        P("seq", "head"),
        P(None, "head"),
        P("head"),
        P("head"),
        P("head", None),
        P(None, None, "head"),
        P("head", None),
        P(None, "head"),
        P("seq", "head"),
        P("seq", "head"),
    )
    out_specs = (
        P("seq", "head"),
        P("seq", "head"),
        P(("seq", "head"), None),
        P(("seq", "head"), None),
        P("seq", "head"),
        P("seq", "head"),
        P("head", None),
        P(None, None, "head"),
        P("head", None),
        P(None, "head"),
    )
    return jax.shard_map(body, mesh=mesh, in_specs=in_specs, out_specs=out_specs, check_vma=False)
```

```python
import jax
import jax.numpy as jnp
from jax import lax
from jax.experimental import pallas as pl
from jax.experimental.pallas import tpu as pltpu
from jax.sharding import PartitionSpec as P

ADAPTER_SCALE = 2.0
NORM_EPS = 1e-05
SIDE = 8
HDIM = 128
NSTATE = 128
TOK = 128
RANK = 32
KCONV = 4
OWN = TOK // SIDE
HALF = NSTATE // 2
SLICE = HALF // SIDE
EARLY = 80
MESH = pl.DeviceIdType.MESH
F32 = jnp.float32
BF16 = jnp.bfloat16


def own_place(kind):
    if kind == "head":
        return lax.axis_index("head")
    seq = lax.axis_index("seq")
    return lax.rem(seq, SIDE) if kind == "z" else seq // SIDE


def along(kind, step):
    if kind == "head":
        place = lax.rem(lax.axis_index("head") + step, SIDE)
        return {"head": place}, place
    seq = lax.axis_index("seq")
    if kind == "seq":
        place = lax.rem(seq + step + SIDE * SIDE, SIDE * SIDE)
        return {"seq": place}, place
    row, col = seq // SIDE, lax.rem(seq, SIDE)
    if kind == "z":
        place = lax.rem(col + step, SIDE)
        return {"seq": row * SIDE + place}, place
    place = lax.rem(row + step, SIDE)
    return {"seq": place * SIDE + col}, place


def send(device, source, target, send_sem, recv_sem):
    copy = pltpu.make_async_remote_copy(
        src_ref=source,
        dst_ref=target,
        send_sem=send_sem,
        recv_sem=recv_sem,
        device_id=device,
        device_id_type=MESH,
    )
    copy.start()
    return copy


class Copies:
    def __init__(self, send_sem, recv_sem):
        self.send_sem, self.recv_sem, self.used, self.all = send_sem, recv_sem, 0, []

    def start(self, device, source, target):
        at = self.used
        self.used += 1
        copy = send(device, source, target, self.send_sem.at[at], self.recv_sem.at[at])
        self.all.append(copy)
        return copy

    def exchange(self, kind, source, target):
        started = []
        for step in range(1, SIDE):
            device, place = along(kind, step)
            started.append(self.start(device, source(place), target))
        return started

    def left(self):
        for copy in self.all:
            copy.wait_send()


def arrived(copies):
    for copy in copies:
        copy.wait_recv()


def nn(a, b):
    return lax.dot_general(a, b, (((1,), (0,)), ((), ())), preferred_element_type=F32)


def nt(a, b):
    return lax.dot_general(a, b, (((1,), (1,)), ((), ())), preferred_element_type=F32)


def split(x):
    high = x.astype(BF16)
    return high, (x - high.astype(F32)).astype(BF16)


def left_exact(a, x, product=nn):
    high, low = split(x)
    return product(a, high) + product(a, low)


def right_exact(x, a, product=nn):
    high, low = split(x)
    return product(high, a) + product(low, a)


def both(x, y, product=nn):
    xh, xl = split(x)
    yh, yl = split(y)
    return product(xh, yh) + (product(xh, yl) + product(xl, yh))


def precise(a, b):
    return lax.dot_general(
        a, b, (((1,), (0,)), ((), ())), precision=lax.Precision.HIGHEST, preferred_element_type=F32
    )


def turned(x):
    missing = 128 - x.shape[1]
    if missing:
        x = jnp.concatenate([x, jnp.zeros((x.shape[0], missing), F32)], axis=1)
    return x.T


def sigmoid(x):
    return 1.0 / (1.0 + jnp.exp(-x))


def lanes(h):
    return pl.ds(pl.multiple_of(h * HDIM, HDIM), HDIM)


def each_head(step):
    lax.fori_loop(0, SIDE, lambda h, c: (step(h), c)[1], 0)


class Fold:
    def __init__(self, copies, refs, reverse):
        self.copies = copies
        (
            self.own, self.row_in, self.row_out, self.row_mix, self.part_out, self.part_in,
            self.enter_out, self.enter_in, self.out,
        ) = refs
        self.order = list(range(SIDE))[::-1] if reverse else list(range(SIDE))
        self.row, self.col = own_place("y"), own_place("z")
        self.flight = [None, None]

    def to_owner(self):
        for half, at in ((0, pl.ds(0, 8 + HALF)), (1, pl.ds(8 + HALF, HALF))):
            self.flight[half] = self.copies.exchange(
                "z", lambda place: self.own.at[place, at], self.row_in.at[self.col, at]
            )
        self.row_in[self.col] = self.own[self.col]

    def to_part(self, half):
        arrived(self.flight[half])
        state = jnp.zeros((HALF, HDIM), F32)
        total = jnp.zeros((8, HDIM), F32)
        for place in self.order:
            self.row_out[half, place] = state
            if half == 0:
                self.row_mix[place] = jnp.exp(total)
            step = self.row_in[place, 0:8]
            total = total + step
            state = (
                jnp.exp(step[0:1]) * state
                + self.row_in[place, 8 + HALF * half : 8 + HALF * (half + 1)]
            )
        for place in range(SIDE):
            self.part_out[half, place, 8 : 8 + SLICE] = state[place * SLICE : (place + 1) * SLICE]
            self.part_out[half, place, 0:8] = total
        self.flight[half] = self.copies.exchange(
            "y",
            lambda place: self.part_out.at[half, place],
            self.part_in.at[half, self.row],
        )
        self.part_in[half, self.row] = self.part_out[half, self.row]

    def to_row(self, half):
        arrived(self.flight[half])
        part = jnp.zeros((SLICE, HDIM), F32)
        for place in self.order:
            self.enter_out[half, place] = part
            decay = jnp.exp(self.part_in[half, place, 0:1])
            part = decay * part + self.part_in[half, place, 8 : 8 + SLICE]
        self.flight[half] = self.copies.exchange(
            "y",
            lambda place: self.enter_out.at[half, place],
            self.enter_in.at[half, self.row],
        )
        self.enter_in[half, self.row] = self.enter_out[half, self.row]

    def to_all(self, half):
        arrived(self.flight[half])
        enter = self.enter_in[half].reshape(HALF, HDIM)
        for place in range(SIDE):
            self.row_out[half, place] = (
                self.row_out[half, place] + self.row_mix[place, 0:1] * enter
            )
        at = pl.ds(HALF * half, HALF)
        self.flight[half] = self.copies.exchange(
            "z", lambda place: self.row_out.at[half, place], self.out.at[self.col, at]
        )
        self.out[self.col, at] = self.row_out[half, self.col]

    def end(self, half):
        arrived(self.flight[half])


def fold_scratch():
    return [
        pltpu.VMEM((SIDE, NSTATE + 8, HDIM), F32),
        pltpu.VMEM((SIDE, NSTATE + 8, HDIM), F32),
        pltpu.VMEM((2, SIDE, HALF, HDIM), F32),
        pltpu.VMEM((SIDE, 8, HDIM), F32),
        pltpu.VMEM((2, SIDE, SLICE + 8, HDIM), F32),
        pltpu.VMEM((2, SIDE, SLICE + 8, HDIM), F32),
        pltpu.VMEM((2, SIDE, SLICE, HDIM), F32),
        pltpu.VMEM((2, SIDE, SLICE, HDIM), F32),
        pltpu.VMEM((SIDE, NSTATE, HDIM), F32),
    ]


class TokenSum:
    def __init__(self, copies, refs, first, second):
        self.copies, self.first, self.second = copies, first, second
        self.own, self.first_in, self.second_out, self.second_in, self.all = refs
        self.part, self.other = own_place(first), own_place(second)

    def to_owner(self):
        self.flight = self.copies.exchange(
            self.first, lambda place: self.own.at[place], self.first_in.at[self.part]
        )
        self.first_in[self.part] = self.own[self.part]

    def to_line(self):
        arrived(self.flight)
        self.second_out[...] = head_total(self.first_in)
        self.flight = self.copies.exchange(
            self.second, lambda place: self.second_out, self.second_in.at[self.other]
        )
        self.second_in[self.other] = self.second_out[...]

    def to_all(self):
        arrived(self.flight)
        self.all[self.part] = head_total(self.second_in)
        self.flight = self.copies.exchange(
            self.first, lambda place: self.all.at[self.part], self.all.at[self.part]
        )

    def end(self):
        arrived(self.flight)


def token_sum_scratch(rows):
    return [
        pltpu.VMEM((SIDE, rows, HDIM), F32),
        pltpu.VMEM((SIDE, rows, HDIM), F32),
        pltpu.VMEM((rows, HDIM), F32),
        pltpu.VMEM((SIDE, rows, HDIM), F32),
        pltpu.VMEM((SIDE, rows, HDIM), F32),
    ]


def head_total(ref):
    total = ref[0]
    for place in range(1, SIDE):
        total = total + ref[place]
    return total


COPIES = 2 + 2 * 8 * 7 + 5 * 7 + 5 * 3 * 7
WIDE = 13
INPUTS = 14


def kernel(*refs):
    refs = list(refs)

    def take(n):
        out = refs[:n]
        del refs[:n]
        return out

    sources = take(INPUTS)
    (skip_ref,) = take(1)
    targets = take(10)
    places = take(INPUTS)
    (x_ref, conv_ref, gate_ref, b_ref, c_ref, l_ref, tap_ref, gain_ref, down_in_ref, up_in_ref,
     down_out_ref, up_out_ref, og_ref, base_ref) = places
    results = take(10)
    (gconv_ref, ggate_ref, gb_ref, gc_ref, gl_ref, glayer_ref, ga_in_ref, gb_in_ref, ga_out_ref,
     gb_out_ref) = results
    fold_refs, back_refs = take(9), take(9)
    early_refs = take(5)
    conv_refs, low_refs = (take(5), take(5)), (take(5), take(5))
    (
        pre3, act3, slope3, y3, outer3, mix3, decay3, weighted3, gs3, dgs3, gssd3, ecum3, toend3,
    ) = take(WIDE)
    (ext, halo, gext, halo_g, first_own, first_all, mid_own, mid_all, out_own, out_all, low_own,
     low_all, bc_own, bc_all, dcum3, gc_acc, gb_acc, dg_acc) = take(18)
    send_sem, recv_sem, load_sem, store_sem = take(4)

    loads = [
        pltpu.make_async_copy(source, place, load_sem.at[i])
        for i, (source, place) in enumerate(zip(sources, places))
    ]
    for load in loads:
        load.start()

    stores = []

    def store(*done):
        for ref in done:
            i = next(i for i, result in enumerate(results) if result is ref)
            copy = pltpu.make_async_copy(ref, targets[i], store_sem.at[i])
            copy.start()
            stores.append(copy)

    seq, head = lax.axis_index("seq"), lax.axis_index("head")
    copies = Copies(send_sem, recv_sem)
    barrier = pltpu.get_barrier_semaphore()
    greeted = 0
    for kind, steps in (
        ("z", range(1, SIDE)), ("y", range(1, SIDE)), ("head", range(1, SIDE)), ("seq", (1, -1))
    ):
        for step in steps:
            pl.semaphore_signal(
                barrier, inc=1, device_id=along(kind, step)[0], device_id_type=MESH
            )
            greeted += 1
    for load in loads:
        load.wait()

    first_own[0:RANK] = nt(up_out_ref[...], og_ref[...])
    first_own[RANK : 2 * RANK] = nt(down_in_ref[...], x_ref[...])
    ext[8 : TOK + 8] = conv_ref[...].astype(F32)

    rows_at = lax.broadcasted_iota(jnp.int32, (TOK, TOK), 0)
    cols_at = lax.broadcasted_iota(jnp.int32, (TOK, TOK), 1)
    causal = rows_at >= cols_at
    cum_turned = precise(l_ref[...], (rows_at <= cols_at).astype(F32))
    cum = turned(jnp.concatenate([cum_turned, jnp.zeros((TOK - SIDE, TOK), F32)], axis=0))
    for h in range(SIDE):
        col = jnp.broadcast_to(cum[:, h : h + 1], (TOK, TOK))
        last = cum[TOK - 1 : TOK, h : h + 1]
        gap = col - cum_turned[h : h + 1]
        decay3[h] = jnp.where(causal, jnp.exp(jnp.where(causal, gap, 0.0)), 0.0)
        ecum3[h] = jnp.exp(col)
        toend3[h] = jnp.exp(jnp.broadcast_to(last, (TOK, TOK)) - col)
        total = jnp.broadcast_to(last, (8, HDIM))
        fold_refs[0][h, 0:8] = total
        back_refs[0][h, 0:8] = total
    b_turned = b_ref[...].astype(F32).T.astype(BF16)
    c_turned = c_ref[...].astype(F32).T.astype(BF16)
    scores = nt(c_ref[...], b_ref[...])
    scores_turned = nt(b_ref[...], c_ref[...])

    pl.semaphore_wait(barrier, greeted)
    tail = copies.start(along("seq", 1)[0], conv_ref.at[TOK - 16 : TOK], halo)
    first = copies.exchange("head", lambda place: first_own, first_all.at[head])
    first_all[head] = first_own[...]

    def gates(h):
        gate = gate_ref[:, lanes(h)].astype(F32)
        sig = sigmoid(gate)
        gs3[h] = gate * sig
        dgs3[h] = sig * (1.0 + gate * (1.0 - sig))

    each_head(gates)

    tail.wait_recv()
    before = halo[...].astype(F32)[8:16]
    ext[0:8] = jnp.where(seq > 0, before, 0.0)

    def local_state(h):
        at = lanes(h)
        taps = tap_ref[:, at].astype(F32)
        pre = ext[5 : 5 + TOK, at] * taps[0:1]
        for k in range(1, KCONV):
            pre = pre + ext[5 + k : 5 + k + TOK, at] * taps[k : k + 1]
        sig = sigmoid(pre)
        act = pre * sig
        act3[h] = act
        slope3[h] = sig * (1.0 + pre * (1.0 - sig))
        fold_refs[0][h, 8 : 8 + NSTATE] = left_exact(b_turned, act * toend3[h])

    each_head(local_state)
    fold = Fold(copies, fold_refs, False)
    fold.to_owner()

    def inner(h):
        mix = decay3[h] * scores
        y3[h] = both(mix, act3[h]) + skip_ref[h] * act3[h]

    each_head(inner)
    fold.to_part(0)
    fold.to_part(1)

    arrived(first)
    sums = head_total(first_all)
    back_out_turned = sums[0:RANK]
    low_in_turned = sums[RANK : 2 * RANK]
    pad = jnp.zeros((TOK - RANK, TOK), F32)
    back_out = turned(jnp.concatenate([back_out_turned, pad], axis=0))[:, 0:RANK]

    def norm_gradient(h):
        at = lanes(h)
        weighted3[h] = (
            base_ref[:, at].astype(F32)
            + ADAPTER_SCALE * right_exact(back_out, down_out_ref[:, at])
        ) * gain_ref[:, at]

    each_head(norm_gradient)
    fold.to_row(0)
    fold.to_row(1)
    fold.to_all(0)
    fold.to_all(1)
    fold.end(0)
    fold.end(1)
    state_in = fold.out

    def gated_sums(h, carry):
        square, dot = carry
        outer = ecum3[h] * left_exact(c_ref[...], state_in[h])
        outer3[h] = outer
        y = y3[h] + outer
        y3[h] = y
        gated = y * gs3[h]
        return square + gated * gated, dot + weighted3[h] * gated

    square, dot = lax.fori_loop(
        0, SIDE, gated_sums, (jnp.zeros((TOK, HDIM), F32), jnp.zeros((TOK, HDIM), F32))
    )
    mid_own[...] = turned(
        jnp.concatenate(
            [
                jnp.sum(square, axis=1, keepdims=True),
                jnp.sum(dot, axis=1, keepdims=True),
                jnp.zeros((TOK, HDIM - 2), F32),
            ],
            axis=1,
        )
    )[0:8]
    mid = copies.exchange("head", lambda place: mid_own, mid_all.at[head])
    mid_all[head] = mid_own[...]

    def project(h, low):
        at = lanes(h)
        return low + left_exact(down_out_ref[:, at], y3[h] * gs3[h] * gain_ref[:, at], nt)

    out_own[...] = lax.fori_loop(0, SIDE, project, jnp.zeros((RANK, TOK), F32))
    out = copies.exchange("head", lambda place: out_own, out_all.at[head])
    out_all[head] = out_own[...]
    arrived(mid)
    sums = head_total(mid_all)
    inv_row = lax.rsqrt(sums[0:1] / (SIDE * SIDE * HDIM) + NORM_EPS)
    kappa_row = inv_row * inv_row * inv_row * sums[1:2] / (SIDE * SIDE * HDIM)
    columns = turned(
        jnp.concatenate([inv_row, kappa_row, jnp.zeros((TOK - 2, TOK), F32)], axis=0)
    )
    inv = jnp.broadcast_to(columns[:, 0:1], (TOK, HDIM))
    kappa = jnp.broadcast_to(columns[:, 1:2], (TOK, HDIM))

    def mixer_gradient(h):
        gated = y3[h] * gs3[h]
        grad_gated = inv * weighted3[h] - gated * kappa
        gssd = grad_gated * gs3[h]
        gssd3[h] = gssd
        pre3[h] = grad_gated * y3[h] * dgs3[h]
        back_refs[0][h, 8 : 8 + NSTATE] = left_exact(c_turned, gssd * ecum3[h])

    each_head(mixer_gradient)
    back = Fold(copies, back_refs, True)
    back.to_owner()

    scale = ADAPTER_SCALE / (SIDE * SIDE * TOK)
    early = TokenSum(copies, early_refs, "y", "z")

    def early_parts(h):
        at = lanes(h)
        ggate = pre3[h]
        ggate_ref[:, at] = ggate.astype(BF16)
        early.own[h, 0:RANK] = scale * both(low_in_turned, ggate)
        normed = y3[h] * gs3[h] * gain_ref[:, at] * inv
        early.own[h, RANK : 2 * RANK] = scale * both(back_out_turned, normed)

    each_head(early_parts)
    arrived(out)
    low_out_turned = head_total(out_all) * inv_row
    grad_b_out = scale * right_exact(low_out_turned, og_ref[...])
    for part in range(SIDE):
        early.own[part, 2 * RANK : 2 * RANK + 16] = grad_b_out[
            16 * (part % 2) : 16 * (part % 2) + 16, HDIM * (part // 2) : HDIM * (part // 2 + 1)
        ]
    store(ggate_ref)
    early.to_owner()

    gc_acc[...] = jnp.zeros((TOK, NSTATE), F32)
    dg_acc[...] = jnp.zeros((TOK, TOK), F32)

    def local_gradient(h):
        gssd = gssd3[h]
        decay = decay3[h]
        part = both(gssd, act3[h], nt) * decay
        dg_acc[...] += part
        moved = part * scores
        dcum3[h] = moved - turned(moved) + gssd * outer3[h]
        mix3[h] = both(turned(decay) * scores_turned, gssd) + skip_ref[h] * gssd
        gc_acc[...] += both(gssd * ecum3[h], state_in[h], nt)

    each_head(local_gradient)
    back.to_part(0)
    back.to_part(1)
    early.to_line()
    dg = dg_acc[...]
    gc_acc[...] += right_exact(dg, b_ref[...])
    gb_acc[...] = right_exact(turned(dg), c_ref[...])
    back.to_row(0)
    back.to_row(1)
    back.to_all(0)
    back.to_all(1)
    early.to_all()
    back.end(0)
    back.end(1)
    state_grad = back.out

    def state_gradient(h):
        toend = toend3[h]
        act = act3[h]
        into = toend * left_exact(b_ref[...], state_grad[h])
        gb_acc[...] += both(act * toend, state_grad[h], nt)
        fell = act * into
        total = jnp.sum(fell, axis=0, keepdims=True) + ecum3[h, TOK - 1 : TOK] * jnp.sum(
            state_in[h] * state_grad[h], axis=0, keepdims=True
        )
        dcum = dcum3[h] - fell
        dcum3[h] = jnp.where(rows_at == TOK - 1, dcum + total, dcum)
        gext[0:TOK, lanes(h)] = (mix3[h] + into) * slope3[h]

    each_head(state_gradient)
    rim = copies.start(along("seq", -1)[0], gext.at[0:8], halo_g)
    for part in range(SIDE):
        bc_own[part, 0:OWN] = gb_acc[OWN * part : OWN * (part + 1)]
        bc_own[part, OWN : 2 * OWN] = gc_acc[OWN * part : OWN * (part + 1)]
    dcum = turned(
        jnp.concatenate(
            [jnp.sum(dcum3[h], axis=1, keepdims=True) for h in range(SIDE)]
            + [jnp.zeros((TOK, HDIM - SIDE), F32)],
            axis=1,
        )
    )[0:SIDE]
    gl_ref[...] = precise(dcum, causal.astype(F32))
    early.end()
    for part in range(SIDE):
        at = slice(HDIM * part, HDIM * (part + 1))
        gb_in_ref[1, :, at] = early.all[part, 0:RANK]
        ga_out_ref[:, at] = early.all[part, RANK : 2 * RANK]
        gb_out_ref[
            16 * (part % 2) : 16 * (part % 2) + 16, HDIM * (part // 2) : HDIM * (part // 2 + 1)
        ] = early.all[part, 2 * RANK : 2 * RANK + 16]
    store(gl_ref, ga_out_ref, gb_out_ref)
    rim.wait_recv()
    gext[TOK : TOK + 8] = jnp.where(seq < SIDE * SIDE - 1, halo_g[...], 0.0)
    axes = (("z", "y"), ("y", "z"))
    conv_sums = [TokenSum(copies, refs, *axis) for refs, axis in zip(conv_refs, axes)]
    low_sums = [TokenSum(copies, refs, *axis) for refs, axis in zip(low_refs, axes)]

    def conv_gradient(h, low):
        at = lanes(h)
        taps = tap_ref[:, at].astype(F32)
        gconv = gext[3 : 3 + TOK, at] * taps[0:1]
        for k in range(1, KCONV):
            gconv = gconv + gext[3 - k : 3 - k + TOK, at] * taps[k : k + 1]
        gconv_ref[:, at] = gconv.astype(BF16)
        grad = scale * both(low_in_turned, gconv)
        conv_sums[0].own[h] = grad[0:16]
        conv_sums[1].own[h] = grad[16:32]
        return low + (
            left_exact(up_in_ref[0, :, at], gconv, nt) + left_exact(up_in_ref[1, :, at], pre3[h], nt)
        )

    low_own[...] = lax.fori_loop(0, SIDE, conv_gradient, jnp.zeros((RANK, TOK), F32))
    store(gconv_ref)
    low = copies.exchange("head", lambda place: low_own, low_all.at[head])
    low_all[head] = low_own[...]
    for sums in conv_sums:
        sums.to_owner()
    arrived(low)
    back_in_turned = head_total(low_all)
    grad_a_in = scale * right_exact(back_in_turned, x_ref[...])
    for part in range(SIDE):
        at = slice(HDIM * (part // 2), HDIM * (part // 2 + 1))
        for sums, first_row in zip(low_sums, (8 * (part % 2), 16 + 8 * (part % 2))):
            sums.own[part] = grad_a_in[first_row : first_row + 8, at]
    for sums in low_sums:
        sums.to_owner()
    rows_out = copies.exchange("head", lambda place: bc_own.at[place], bc_all.at[head])
    bc_all[head] = bc_own[head]
    back_in = turned(jnp.concatenate([back_in_turned, pad], axis=0))[:, 0:RANK]
    glayer_ref[...] = (ADAPTER_SCALE * right_exact(back_in, down_in_ref[...])).astype(BF16)
    for sums in conv_sums + low_sums:
        sums.to_line()
    arrived(rows_out)
    sums = head_total(bc_all)
    gb_ref[...] = sums[0:OWN]
    gc_ref[...] = sums[OWN : 2 * OWN]
    store(glayer_ref, gb_ref, gc_ref)
    for sums in conv_sums + low_sums:
        sums.to_all()
    for sums in conv_sums + low_sums:
        sums.end()
    for part in range(SIDE):
        at = slice(HDIM * part, HDIM * (part + 1))
        gb_in_ref[0, 0:16, at] = conv_sums[0].all[part]
        gb_in_ref[0, 16:32, at] = conv_sums[1].all[part]
        at = slice(HDIM * (part // 2), HDIM * (part // 2 + 1))
        for sums, first_row in zip(low_sums, (8 * (part % 2), 16 + 8 * (part % 2))):
            ga_in_ref[first_row : first_row + 8, at] = sums.all[part]
    store(gb_in_ref, ga_in_ref)
    copies.left()
    for copy in stores:
        copy.wait()


def hand_over(*refs):
    count = (len(refs) - 2) // 3
    sources, targets, places = refs[:count], refs[count : 2 * count], refs[2 * count : 3 * count]
    load_sem, store_sem = refs[-2:]
    loads = [
        pltpu.make_async_copy(sources[i], places[i], load_sem.at[i]) for i in range(count)
    ]
    stores = [
        pltpu.make_async_copy(places[i], targets[i], store_sem.at[i]) for i in range(count)
    ]
    for load in loads:
        load.start()
    for load, store in zip(loads, stores):
        load.wait()
        store.start()
    for store in stores:
        store.wait()


def body(x, conv, gate, b, c, l, taps, skip, gain, down_in, up_in, down_out, up_out, og, base):
    wide = conv.shape[1]
    inputs = (
        x, conv, gate, b, c, l.T, taps, gain.reshape(1, wide), down_in.T, up_in, down_out.T,
        up_out, og, base,
    )
    outs = [
        jax.ShapeDtypeStruct(conv.shape, BF16),
        jax.ShapeDtypeStruct(gate.shape, BF16),
        jax.ShapeDtypeStruct((OWN, NSTATE), F32),
        jax.ShapeDtypeStruct((OWN, NSTATE), F32),
        jax.ShapeDtypeStruct(l.shape[::-1], F32),
        jax.ShapeDtypeStruct(x.shape, BF16),
        jax.ShapeDtypeStruct(down_in.shape[::-1], F32),
        jax.ShapeDtypeStruct(up_in.shape, F32),
        jax.ShapeDtypeStruct(down_out.shape[::-1], F32),
        jax.ShapeDtypeStruct(up_out.shape, F32),
    ]
    in_place = [pl.BlockSpec(memory_space=pl.ANY) for _ in outs]
    results = pl.pallas_call(
        kernel,
        out_shape=outs,
        in_specs=[pl.BlockSpec(memory_space=pl.ANY) for _ in inputs]
        + [pl.BlockSpec(memory_space=pltpu.SMEM)],
        out_specs=in_place,
        scratch_shapes=[pltpu.VMEM(a.shape, a.dtype) for a in inputs]
        + [pltpu.VMEM(a.shape, a.dtype) for a in outs]
        + fold_scratch()
        + fold_scratch()
        + token_sum_scratch(EARLY)
        + token_sum_scratch(16)
        + token_sum_scratch(16)
        + token_sum_scratch(8)
        + token_sum_scratch(8)
        + [pltpu.VMEM((SIDE, TOK, HDIM), F32) for _ in range(WIDE)]
        + [
            pltpu.VMEM((TOK + 8, wide), F32),
            pltpu.VMEM((16, wide), BF16),
            pltpu.VMEM((TOK + 8, wide), F32),
            pltpu.VMEM((8, wide), F32),
            pltpu.VMEM((2 * RANK, TOK), F32),
            pltpu.VMEM((SIDE, 2 * RANK, TOK), F32),
            pltpu.VMEM((8, TOK), F32),
            pltpu.VMEM((SIDE, 8, TOK), F32),
            pltpu.VMEM((RANK, TOK), F32),
            pltpu.VMEM((SIDE, RANK, TOK), F32),
            pltpu.VMEM((RANK, TOK), F32),
            pltpu.VMEM((SIDE, RANK, TOK), F32),
            pltpu.VMEM((SIDE, 2 * OWN, NSTATE), F32),
            pltpu.VMEM((SIDE, 2 * OWN, NSTATE), F32),
            pltpu.VMEM((SIDE, TOK, HDIM), F32),
            pltpu.VMEM((TOK, NSTATE), F32),
            pltpu.VMEM((TOK, NSTATE), F32),
            pltpu.VMEM((TOK, TOK), F32),
            pltpu.SemaphoreType.DMA((COPIES,)),
            pltpu.SemaphoreType.DMA((COPIES,)),
            pltpu.SemaphoreType.DMA((INPUTS,)),
            pltpu.SemaphoreType.DMA((len(outs),)),
        ],
        compiler_params=pltpu.CompilerParams(
            collective_id=0, has_side_effects=True, vmem_limit_bytes=60 << 20
        ),
    )(*inputs, skip)
    results = pl.pallas_call(
        hand_over,
        out_shape=outs,
        in_specs=in_place,
        out_specs=in_place,
        scratch_shapes=[pltpu.VMEM(a.shape, a.dtype) for a in outs]
        + [pltpu.SemaphoreType.DMA((len(outs),)), pltpu.SemaphoreType.DMA((len(outs),))],
        compiler_params=pltpu.CompilerParams(vmem_limit_bytes=60 << 20),
    )(*results)
    turn = (4, 6, 8)
    return tuple(r.T if i in turn else r for i, r in enumerate(results))


def solution(mesh):
    in_specs = (
        P("seq", "head"),
        P("seq", "head"),
        P("seq", "head"),
        P("seq", None),
        P("seq", None),
        P("seq", "head"),
        P(None, "head"),
        P("head"),
        P("head"),
        P("head", None),
        P(None, None, "head"),
        P("head", None),
        P(None, "head"),
        P("seq", "head"),
        P("seq", "head"),
    )
    out_specs = (
        P("seq", "head"),
        P("seq", "head"),
        P(("seq", "head"), None),
        P(("seq", "head"), None),
        P("seq", "head"),
        P("seq", "head"),
        P("head", None),
        P(None, None, "head"),
        P("head", None),
        P(None, "head"),
    )
    return jax.shard_map(body, mesh=mesh, in_specs=in_specs, out_specs=out_specs, check_vma=False)
```

```python
import jax
import jax.numpy as jnp
from jax import lax
from jax.experimental import pallas as pl
from jax.experimental.pallas import tpu as pltpu
from jax.sharding import PartitionSpec as P

ADAPTER_SCALE = 2.0
NORM_EPS = 1e-05
SIDE = 8
HDIM = 128
NSTATE = 128
TOK = 128
RANK = 32
KCONV = 4
OWN = TOK // SIDE
CHUNKS = 4
ROWS = NSTATE // CHUNKS
EARLY = 80
MESH = pl.DeviceIdType.MESH
F32 = jnp.float32
BF16 = jnp.bfloat16


def own_place(kind):
    if kind == "head":
        return lax.axis_index("head")
    seq = lax.axis_index("seq")
    return lax.rem(seq, SIDE) if kind == "z" else seq // SIDE


def along(kind, step):
    if kind == "head":
        place = lax.rem(lax.axis_index("head") + step, SIDE)
        return {"head": place}, place
    seq = lax.axis_index("seq")
    if kind == "seq":
        place = lax.rem(seq + step + SIDE * SIDE, SIDE * SIDE)
        return {"seq": place}, place
    row, col = seq // SIDE, lax.rem(seq, SIDE)
    if kind == "z":
        place = lax.rem(col + step, SIDE)
        return {"seq": row * SIDE + place}, place
    place = lax.rem(row + step, SIDE)
    return {"seq": place * SIDE + col}, place


def send(device, source, target, send_sem, recv_sem):
    copy = pltpu.make_async_remote_copy(
        src_ref=source,
        dst_ref=target,
        send_sem=send_sem,
        recv_sem=recv_sem,
        device_id=device,
        device_id_type=MESH,
    )
    copy.start()
    return copy


class Copies:
    def __init__(self, send_sem, recv_sem):
        self.send_sem, self.recv_sem, self.used, self.all = send_sem, recv_sem, 0, []

    def start(self, device, source, target):
        at = self.used
        self.used += 1
        copy = send(device, source, target, self.send_sem.at[at], self.recv_sem.at[at])
        self.all.append(copy)
        return copy

    def exchange(self, kind, source, target):
        started = []
        for step in range(1, SIDE):
            device, place = along(kind, step)
            started.append(self.start(device, source(place), target))
        return started

    def left(self):
        for copy in self.all:
            copy.wait_send()


def arrived(copies):
    for copy in copies:
        copy.wait_recv()


def nn(a, b):
    return lax.dot_general(a, b, (((1,), (0,)), ((), ())), preferred_element_type=F32)


def nt(a, b):
    return lax.dot_general(a, b, (((1,), (1,)), ((), ())), preferred_element_type=F32)


def split(x):
    high = x.astype(BF16)
    return high, (x - high.astype(F32)).astype(BF16)


def left_exact(a, x, product=nn):
    high, low = split(x)
    return product(a, high) + product(a, low)


def right_exact(x, a, product=nn):
    high, low = split(x)
    return product(high, a) + product(low, a)


def both(x, y, product=nn):
    xh, xl = split(x)
    yh, yl = split(y)
    return product(xh, yh) + (product(xh, yl) + product(xl, yh))


def precise(a, b):
    return lax.dot_general(
        a, b, (((1,), (0,)), ((), ())), precision=lax.Precision.HIGHEST, preferred_element_type=F32
    )


def turned(x):
    missing = 128 - x.shape[1]
    if missing:
        x = jnp.concatenate([x, jnp.zeros((x.shape[0], missing), F32)], axis=1)
    return x.T


def sigmoid(x):
    return 1.0 / (1.0 + jnp.exp(-x))


def lanes(h):
    return pl.ds(pl.multiple_of(h * HDIM, HDIM), HDIM)


def each_head(step):
    lax.fori_loop(0, SIDE, lambda h, c: (step(h), c)[1], 0)


class Fold:
    def __init__(self, copies, refs, reverse):
        self.copies = copies
        (
            self.own, self.row_in, self.row_out, self.row_mix, self.part_out, self.part_in,
            self.out,
        ) = refs
        self.order = list(range(SIDE))[::-1] if reverse else list(range(SIDE))
        self.row, self.col = own_place("y"), own_place("z")
        self.flight = [[] for _ in range(CHUNKS)]

    def to_owner(self, chunk, step):
        at = pl.ds(8 + ROWS * chunk, ROWS) if chunk else pl.ds(0, 8 + ROWS)
        if step == SIDE:
            self.row_in[self.col, at] = self.own[self.col, at]
            return
        device, place = along("z", step)
        self.flight[chunk].append(
            self.copies.start(device, self.own.at[place, at], self.row_in.at[self.col, at])
        )

    def to_column(self, chunk):
        arrived(self.flight[chunk])
        state = jnp.zeros((ROWS, HDIM), F32)
        total = jnp.zeros((8, HDIM), F32)
        for place in self.order:
            self.row_out[chunk, place] = state
            if chunk == 0:
                self.row_mix[place] = jnp.exp(total)
            step = self.row_in[place, 0:8]
            total = total + step
            state = (
                jnp.exp(step[0:1]) * state
                + self.row_in[place, 8 + ROWS * chunk : 8 + ROWS * (chunk + 1)]
            )
        self.part_out[chunk, 0:8] = total
        self.part_out[chunk, 8 : 8 + ROWS] = state
        self.flight[chunk] = self.copies.exchange(
            "y", lambda place: self.part_out.at[chunk], self.part_in.at[chunk, self.row]
        )
        self.part_in[chunk, self.row] = self.part_out[chunk]

    def to_all(self, chunk):
        arrived(self.flight[chunk])
        part = jnp.zeros((ROWS, HDIM), F32)
        enter = part
        for place in self.order:
            enter = jnp.where(self.row == place, part, enter)
            decay = jnp.exp(self.part_in[chunk, place, 0:1])
            part = decay * part + self.part_in[chunk, place, 8 : 8 + ROWS]
        for place in range(SIDE):
            self.row_out[chunk, place] = (
                self.row_out[chunk, place] + self.row_mix[place, 0:1] * enter
            )
        at = pl.ds(ROWS * chunk, ROWS)
        self.flight[chunk] = self.copies.exchange(
            "z", lambda place: self.row_out.at[chunk, place], self.out.at[self.col, at]
        )
        self.out[self.col, at] = self.row_out[chunk, self.col]

    def end(self, step):
        for flight in self.flight:
            if step:
                flight[step - 1].wait_recv()
        return lax.rem(self.col - step + SIDE, SIDE)


NEAREST = (0, 1, 7, 2, 6, 3, 5, 4)


def fold_scratch():
    return [
        pltpu.VMEM((SIDE, NSTATE + 8, HDIM), F32),
        pltpu.VMEM((SIDE, NSTATE + 8, HDIM), F32),
        pltpu.VMEM((CHUNKS, SIDE, ROWS, HDIM), F32),
        pltpu.VMEM((SIDE, 8, HDIM), F32),
        pltpu.VMEM((CHUNKS, ROWS + 8, HDIM), F32),
        pltpu.VMEM((CHUNKS, SIDE, ROWS + 8, HDIM), F32),
        pltpu.VMEM((SIDE, NSTATE, HDIM), F32),
    ]


class TokenSum:
    def __init__(self, copies, refs, first, second):
        self.copies, self.first, self.second = copies, first, second
        self.own, self.first_in, self.second_out, self.second_in, self.all = refs
        self.part, self.other = own_place(first), own_place(second)

    def to_owner(self):
        self.flight = self.copies.exchange(
            self.first, lambda place: self.own.at[place], self.first_in.at[self.part]
        )
        self.first_in[self.part] = self.own[self.part]

    def to_line(self):
        arrived(self.flight)
        self.second_out[...] = head_total(self.first_in)
        self.flight = self.copies.exchange(
            self.second, lambda place: self.second_out, self.second_in.at[self.other]
        )
        self.second_in[self.other] = self.second_out[...]

    def to_all(self):
        arrived(self.flight)
        self.all[self.part] = head_total(self.second_in)
        self.flight = self.copies.exchange(
            self.first, lambda place: self.all.at[self.part], self.all.at[self.part]
        )

    def end(self):
        arrived(self.flight)


def token_sum_scratch(rows):
    return [
        pltpu.VMEM((SIDE, rows, HDIM), F32),
        pltpu.VMEM((SIDE, rows, HDIM), F32),
        pltpu.VMEM((rows, HDIM), F32),
        pltpu.VMEM((SIDE, rows, HDIM), F32),
        pltpu.VMEM((SIDE, rows, HDIM), F32),
    ]


def head_total(ref):
    total = ref[0]
    for place in range(1, SIDE):
        total = total + ref[place]
    return total


COPIES = 2 + 2 * 3 * CHUNKS * 7 + 5 * 7 + 5 * 3 * 7
WIDE = 13
INPUTS = 14
FETCH_ORDER = (1, 5, 3, 6, 11, 12, 8, 0, 4, 2, 13, 10, 7, 9)


def kernel(*refs):
    refs = list(refs)

    def take(n):
        out = refs[:n]
        del refs[:n]
        return out

    sources = take(INPUTS)
    (skip_ref,) = take(1)
    targets = take(10)
    places = take(INPUTS)
    (x_ref, conv_ref, gate_ref, b_ref, c_ref, l_ref, tap_ref, gain_ref, down_in_ref, up_in_ref,
     down_out_ref, up_out_ref, og_ref, base_ref) = places
    results = take(10)
    (gconv_ref, ggate_ref, gb_ref, gc_ref, gl_ref, glayer_ref, ga_in_ref, gb_in_ref, ga_out_ref,
     gb_out_ref) = results
    fold_refs, back_refs = take(7), take(7)
    early_refs = take(5)
    conv_refs, low_refs = (take(5), take(5)), (take(5), take(5))
    (
        pre3, act3, slope3, y3, outer3, mix3, decay3, weighted3, gs3, dgs3, gssd3, ecum3, toend3,
    ) = take(WIDE)
    (ext, halo, gext, halo_g, first_own, first_all, mid_own, mid_all, out_own, out_all, low_own,
     low_all, bc_own, bc_all, dcum3, gc_acc, gb_acc, dg_acc, rim_own) = take(19)
    send_sem, recv_sem, load_sem, store_sem = take(4)

    stores = []

    def store(*done):
        for ref in done:
            i = next(i for i, result in enumerate(results) if result is ref)
            copy = pltpu.make_async_copy(ref, targets[i], store_sem.at[i])
            copy.start()
            stores.append(copy)

    seq, head = lax.axis_index("seq"), lax.axis_index("head")
    copies = Copies(send_sem, recv_sem)
    barrier = pltpu.get_barrier_semaphore()
    greeted = 0
    for kind, steps in (
        ("seq", (1, -1)), ("z", range(1, SIDE)), ("y", range(1, SIDE)), ("head", range(1, SIDE))
    ):
        for step in steps:
            pl.semaphore_signal(
                barrier, inc=1, device_id=along(kind, step)[0], device_id_type=MESH
            )
            greeted += 1
    loads = {}
    for i in FETCH_ORDER:
        loads[i] = pltpu.make_async_copy(sources[i], places[i], load_sem.at[i])
        loads[i].start()

    def fetched(*which):
        for ref in which:
            loads[next(i for i, place in enumerate(places) if place is ref)].wait()

    fetched(conv_ref)
    pl.semaphore_wait(barrier, greeted)
    tail = copies.start(along("seq", 1)[0], conv_ref.at[TOK - 16 : TOK], halo)
    ext[8 : TOK + 8] = conv_ref[...].astype(F32)
    rows_at = lax.broadcasted_iota(jnp.int32, (TOK, TOK), 0)
    cols_at = lax.broadcasted_iota(jnp.int32, (TOK, TOK), 1)
    causal = rows_at >= cols_at
    fetched(l_ref, b_ref, tap_ref)
    cum_turned = precise(l_ref[...], (rows_at <= cols_at).astype(F32))
    cum = turned(jnp.concatenate([cum_turned, jnp.zeros((TOK - SIDE, TOK), F32)], axis=0))
    for h in range(SIDE):
        last = cum[TOK - 1 : TOK, h : h + 1]
        toend3[h] = jnp.exp(jnp.broadcast_to(last - cum[:, h : h + 1], (TOK, TOK)))
        total = jnp.broadcast_to(last, (8, HDIM))
        fold_refs[0][h, 0:8] = total
        back_refs[0][h, 0:8] = total
    b_turned = b_ref[...].astype(F32).T.astype(BF16)
    tail.wait_recv()
    before = halo[...].astype(F32)[8:16]
    ext[0:8] = jnp.where(seq > 0, before, 0.0)
    fold = Fold(copies, fold_refs, False)

    def local_state(h):
        at = lanes(h)
        taps = tap_ref[:, at].astype(F32)
        pre = ext[5 : 5 + TOK, at] * taps[0:1]
        for k in range(1, KCONV):
            pre = pre + ext[5 + k : 5 + k + TOK, at] * taps[k : k + 1]
        sig = sigmoid(pre)
        act = pre * sig
        act3[h] = act
        slope3[h] = sig * (1.0 + pre * (1.0 - sig))
        fold.own[h, 8 : 8 + NSTATE] = left_exact(b_turned, act * toend3[h])

    for step in range(1, SIDE + 1):
        local_state(lax.rem(fold.col + step, SIDE))
        fold.to_owner(0, step)
    for chunk in range(1, CHUNKS):
        for step in range(1, SIDE + 1):
            fold.to_owner(chunk, step)

    fetched(up_out_ref, og_ref, down_in_ref, x_ref)
    first_own[0:RANK] = nt(up_out_ref[...], og_ref[...])
    first_own[RANK : 2 * RANK] = nt(down_in_ref[...], x_ref[...])
    first = copies.exchange("head", lambda place: first_own, first_all.at[head])
    first_all[head] = first_own[...]

    for h in range(SIDE):
        col = jnp.broadcast_to(cum[:, h : h + 1], (TOK, TOK))
        gap = col - cum_turned[h : h + 1]
        decay3[h] = jnp.where(causal, jnp.exp(jnp.where(causal, gap, 0.0)), 0.0)
        ecum3[h] = jnp.exp(col)
    fetched(c_ref, gate_ref)
    c_turned = c_ref[...].astype(F32).T.astype(BF16)
    scores = nt(c_ref[...], b_ref[...])
    scores_turned = nt(b_ref[...], c_ref[...])

    def inner(h):
        mix = decay3[h] * scores
        y3[h] = both(mix, act3[h]) + skip_ref[h] * act3[h]
        gate = gate_ref[:, lanes(h)].astype(F32)
        sig = sigmoid(gate)
        gs3[h] = gate * sig
        dgs3[h] = sig * (1.0 + gate * (1.0 - sig))

    fold.to_column(0)
    each_head(inner)
    fold.to_column(1)

    arrived(first)
    fetched(base_ref, down_out_ref, gain_ref, up_in_ref)
    sums = head_total(first_all)
    back_out_turned = sums[0:RANK]
    low_in_turned = sums[RANK : 2 * RANK]
    pad = jnp.zeros((TOK - RANK, TOK), F32)
    back_out = turned(jnp.concatenate([back_out_turned, pad], axis=0))[:, 0:RANK]

    def norm_gradient(h):
        at = lanes(h)
        weighted3[h] = (
            base_ref[:, at].astype(F32)
            + ADAPTER_SCALE * right_exact(back_out, down_out_ref[:, at])
        ) * gain_ref[:, at]

    each_head(norm_gradient)
    for chunk in range(2, CHUNKS):
        fold.to_column(chunk)
    for chunk in range(CHUNKS):
        fold.to_all(chunk)
    state_in = fold.out

    square, dot = jnp.zeros((TOK, HDIM), F32), jnp.zeros((TOK, HDIM), F32)
    for step in NEAREST:
        h = fold.end(step)
        outer = ecum3[h] * left_exact(c_ref[...], state_in[h])
        outer3[h] = outer
        y = y3[h] + outer
        y3[h] = y
        gated = y * gs3[h]
        square = square + gated * gated
        dot = dot + weighted3[h] * gated
    mid_own[...] = turned(
        jnp.concatenate(
            [
                jnp.sum(square, axis=1, keepdims=True),
                jnp.sum(dot, axis=1, keepdims=True),
                jnp.zeros((TOK, HDIM - 2), F32),
            ],
            axis=1,
        )
    )[0:8]
    mid = copies.exchange("head", lambda place: mid_own, mid_all.at[head])
    mid_all[head] = mid_own[...]

    def project(h, low):
        at = lanes(h)
        return low + left_exact(down_out_ref[:, at], y3[h] * gs3[h] * gain_ref[:, at], nt)

    out_own[...] = lax.fori_loop(0, SIDE, project, jnp.zeros((RANK, TOK), F32))
    out = copies.exchange("head", lambda place: out_own, out_all.at[head])
    out_all[head] = out_own[...]
    arrived(mid)
    sums = head_total(mid_all)
    inv_row = lax.rsqrt(sums[0:1] / (SIDE * SIDE * HDIM) + NORM_EPS)
    kappa_row = inv_row * inv_row * inv_row * sums[1:2] / (SIDE * SIDE * HDIM)
    columns = turned(
        jnp.concatenate([inv_row, kappa_row, jnp.zeros((TOK - 2, TOK), F32)], axis=0)
    )
    inv = jnp.broadcast_to(columns[:, 0:1], (TOK, HDIM))
    kappa = jnp.broadcast_to(columns[:, 1:2], (TOK, HDIM))

    def mixer_gradient(h):
        gated = y3[h] * gs3[h]
        grad_gated = inv * weighted3[h] - gated * kappa
        gssd = grad_gated * gs3[h]
        gssd3[h] = gssd
        pre3[h] = grad_gated * y3[h] * dgs3[h]
        back.own[h, 8 : 8 + NSTATE] = left_exact(c_turned, gssd * ecum3[h])

    back = Fold(copies, back_refs, True)
    for step in range(1, SIDE + 1):
        mixer_gradient(lax.rem(back.col + step, SIDE))
        back.to_owner(0, step)
    for chunk in range(1, CHUNKS):
        for step in range(1, SIDE + 1):
            back.to_owner(chunk, step)

    scale = ADAPTER_SCALE / (SIDE * SIDE * TOK)
    early = TokenSum(copies, early_refs, "z", "y")

    def early_parts(h, low):
        at = lanes(h)
        ggate = pre3[h]
        ggate_ref[:, at] = ggate.astype(BF16)
        early.own[h, 0:RANK] = scale * both(low_in_turned, ggate)
        normed = y3[h] * gs3[h] * gain_ref[:, at] * inv
        early.own[h, RANK : 2 * RANK] = scale * both(back_out_turned, normed)
        return low + left_exact(up_in_ref[1, :, at], ggate, nt)

    low_gate = lax.fori_loop(0, SIDE, early_parts, jnp.zeros((RANK, TOK), F32))
    arrived(out)
    low_out_turned = head_total(out_all) * inv_row
    grad_b_out = scale * right_exact(low_out_turned, og_ref[...])
    for part in range(SIDE):
        early.own[part, 2 * RANK : 2 * RANK + 16] = grad_b_out[
            16 * (part % 2) : 16 * (part % 2) + 16, HDIM * (part // 2) : HDIM * (part // 2 + 1)
        ]
    store(ggate_ref)
    early.to_owner()

    gc_acc[...] = jnp.zeros((TOK, NSTATE), F32)
    dg_acc[...] = jnp.zeros((TOK, TOK), F32)

    def local_gradient(h):
        gssd = gssd3[h]
        decay = decay3[h]
        part = both(gssd, act3[h], nt) * decay
        dg_acc[...] += part
        moved = part * scores
        dcum3[h] = moved - turned(moved) + gssd * outer3[h]
        mix3[h] = both(turned(decay) * scores_turned, gssd) + skip_ref[h] * gssd
        gc_acc[...] += both(gssd * ecum3[h], state_in[h], nt)

    lax.fori_loop(0, SIDE // 2, lambda h, c: (local_gradient(h), c)[1], 0)
    back.to_column(0)
    lax.fori_loop(SIDE // 2, SIDE, lambda h, c: (local_gradient(h), c)[1], 0)
    for chunk in range(1, CHUNKS):
        back.to_column(chunk)
    dg = dg_acc[...]
    gc_acc[...] += right_exact(dg, b_ref[...])
    gb_acc[...] = right_exact(turned(dg), c_ref[...])
    for chunk in range(CHUNKS - 1):
        back.to_all(chunk)
    back.to_all(CHUNKS - 1)
    early.to_line()
    state_grad = back.out

    for step in NEAREST:
        h = back.end(step)
        into = toend3[h, 0:8] * left_exact(b_ref[0:16], state_grad[h])[0:8]
        rim_own[:, lanes(h)] = (mix3[h, 0:8] + into) * slope3[h, 0:8]
    rim = copies.start(along("seq", -1)[0], rim_own, halo_g)

    def state_gradient(h):
        toend = toend3[h]
        act = act3[h]
        into = toend * left_exact(b_ref[...], state_grad[h])
        gb_acc[...] += both(act * toend, state_grad[h], nt)
        fell = act * into
        total = jnp.sum(fell, axis=0, keepdims=True) + ecum3[h, TOK - 1 : TOK] * jnp.sum(
            state_in[h] * state_grad[h], axis=0, keepdims=True
        )
        dcum = dcum3[h] - fell
        dcum3[h] = jnp.where(rows_at == TOK - 1, dcum + total, dcum)
        gext[0:TOK, lanes(h)] = (mix3[h] + into) * slope3[h]

    each_head(state_gradient)
    early.to_all()
    rim.wait_recv()
    gext[TOK : TOK + 8] = jnp.where(seq < SIDE * SIDE - 1, halo_g[...], 0.0)
    axes = (("z", "y"), ("y", "z"))
    conv_sums = [TokenSum(copies, refs, *axis) for refs, axis in zip(conv_refs, axes)]
    low_sums = [TokenSum(copies, refs, *axis) for refs, axis in zip(low_refs, axes)]

    def conv_gradient(h, low):
        at = lanes(h)
        taps = tap_ref[:, at].astype(F32)
        gconv = gext[3 : 3 + TOK, at] * taps[0:1]
        for k in range(1, KCONV):
            gconv = gconv + gext[3 - k : 3 - k + TOK, at] * taps[k : k + 1]
        gconv_ref[:, at] = gconv.astype(BF16)
        y3[h] = gconv
        return low + left_exact(up_in_ref[0, :, at], gconv, nt)

    low_own[...] = lax.fori_loop(0, SIDE, conv_gradient, low_gate)
    low = copies.exchange("head", lambda place: low_own, low_all.at[head])
    low_all[head] = low_own[...]

    def conv_parts(h):
        grad = scale * both(low_in_turned, y3[h])
        conv_sums[0].own[h] = grad[0:16]
        conv_sums[1].own[h] = grad[16:32]

    each_head(conv_parts)
    for sums in conv_sums:
        sums.to_owner()
    store(gconv_ref)
    dcum = turned(
        jnp.concatenate(
            [jnp.sum(dcum3[h], axis=1, keepdims=True) for h in range(SIDE)]
            + [jnp.zeros((TOK, HDIM - SIDE), F32)],
            axis=1,
        )
    )[0:SIDE]
    gl_ref[...] = precise(dcum, causal.astype(F32))
    store(gl_ref)
    arrived(low)
    back_in_turned = head_total(low_all)
    grad_a_in = scale * right_exact(back_in_turned, x_ref[...])
    for part in range(SIDE):
        at = slice(HDIM * (part // 2), HDIM * (part // 2 + 1))
        for sums, first_row in zip(low_sums, (8 * (part % 2), 16 + 8 * (part % 2))):
            sums.own[part] = grad_a_in[first_row : first_row + 8, at]
    for sums in low_sums:
        sums.to_owner()
    for part in range(SIDE):
        bc_own[part, 0:OWN] = gb_acc[OWN * part : OWN * (part + 1)]
        bc_own[part, OWN : 2 * OWN] = gc_acc[OWN * part : OWN * (part + 1)]
    rows_out = copies.exchange("head", lambda place: bc_own.at[place], bc_all.at[head])
    bc_all[head] = bc_own[head]
    back_in = turned(jnp.concatenate([back_in_turned, pad], axis=0))[:, 0:RANK]
    glayer_ref[...] = (ADAPTER_SCALE * right_exact(back_in, down_in_ref[...])).astype(BF16)
    for sums in conv_sums + low_sums:
        sums.to_line()
    early.end()
    for part in range(SIDE):
        at = slice(HDIM * part, HDIM * (part + 1))
        gb_in_ref[1, :, at] = early.all[part, 0:RANK]
        ga_out_ref[:, at] = early.all[part, RANK : 2 * RANK]
        gb_out_ref[
            16 * (part % 2) : 16 * (part % 2) + 16, HDIM * (part // 2) : HDIM * (part // 2 + 1)
        ] = early.all[part, 2 * RANK : 2 * RANK + 16]
    store(ga_out_ref, gb_out_ref)
    arrived(rows_out)
    sums = head_total(bc_all)
    gb_ref[...] = sums[0:OWN]
    gc_ref[...] = sums[OWN : 2 * OWN]
    store(glayer_ref, gb_ref, gc_ref)
    for sums in conv_sums + low_sums:
        sums.to_all()
    for sums in conv_sums + low_sums:
        sums.end()
    for part in range(SIDE):
        at = slice(HDIM * part, HDIM * (part + 1))
        gb_in_ref[0, 0:16, at] = conv_sums[0].all[part]
        gb_in_ref[0, 16:32, at] = conv_sums[1].all[part]
        at = slice(HDIM * (part // 2), HDIM * (part // 2 + 1))
        for sums, first_row in zip(low_sums, (8 * (part % 2), 16 + 8 * (part % 2))):
            ga_in_ref[first_row : first_row + 8, at] = sums.all[part]
    store(gb_in_ref, ga_in_ref)
    copies.left()
    for copy in stores:
        copy.wait()


def hand_over(*refs):
    count = (len(refs) - 2) // 3
    sources, targets, places = refs[:count], refs[count : 2 * count], refs[2 * count : 3 * count]
    load_sem, store_sem = refs[-2:]
    loads = [
        pltpu.make_async_copy(sources[i], places[i], load_sem.at[i]) for i in range(count)
    ]
    stores = [
        pltpu.make_async_copy(places[i], targets[i], store_sem.at[i]) for i in range(count)
    ]
    for load in loads:
        load.start()
    for load, store in zip(loads, stores):
        load.wait()
        store.start()
    for store in stores:
        store.wait()


def body(x, conv, gate, b, c, l, taps, skip, gain, down_in, up_in, down_out, up_out, og, base):
    wide = conv.shape[1]
    inputs = (
        x, conv, gate, b, c, l.T, taps, gain.reshape(1, wide), down_in.T, up_in, down_out.T,
        up_out, og, base,
    )
    outs = [
        jax.ShapeDtypeStruct(conv.shape, BF16),
        jax.ShapeDtypeStruct(gate.shape, BF16),
        jax.ShapeDtypeStruct((OWN, NSTATE), F32),
        jax.ShapeDtypeStruct((OWN, NSTATE), F32),
        jax.ShapeDtypeStruct(l.shape[::-1], F32),
        jax.ShapeDtypeStruct(x.shape, BF16),
        jax.ShapeDtypeStruct(down_in.shape[::-1], F32),
        jax.ShapeDtypeStruct(up_in.shape, F32),
        jax.ShapeDtypeStruct(down_out.shape[::-1], F32),
        jax.ShapeDtypeStruct(up_out.shape, F32),
    ]
    in_place = [pl.BlockSpec(memory_space=pl.ANY) for _ in outs]
    results = pl.pallas_call(
        kernel,
        out_shape=outs,
        in_specs=[pl.BlockSpec(memory_space=pl.ANY) for _ in inputs]
        + [pl.BlockSpec(memory_space=pltpu.SMEM)],
        out_specs=in_place,
        scratch_shapes=[pltpu.VMEM(a.shape, a.dtype) for a in inputs]
        + [pltpu.VMEM(a.shape, a.dtype) for a in outs]
        + fold_scratch()
        + fold_scratch()
        + token_sum_scratch(EARLY)
        + token_sum_scratch(16)
        + token_sum_scratch(16)
        + token_sum_scratch(8)
        + token_sum_scratch(8)
        + [pltpu.VMEM((SIDE, TOK, HDIM), F32) for _ in range(WIDE)]
        + [
            pltpu.VMEM((TOK + 8, wide), F32),
            pltpu.VMEM((16, wide), BF16),
            pltpu.VMEM((TOK + 8, wide), F32),
            pltpu.VMEM((8, wide), F32),
            pltpu.VMEM((2 * RANK, TOK), F32),
            pltpu.VMEM((SIDE, 2 * RANK, TOK), F32),
            pltpu.VMEM((8, TOK), F32),
            pltpu.VMEM((SIDE, 8, TOK), F32),
            pltpu.VMEM((RANK, TOK), F32),
            pltpu.VMEM((SIDE, RANK, TOK), F32),
            pltpu.VMEM((RANK, TOK), F32),
            pltpu.VMEM((SIDE, RANK, TOK), F32),
            pltpu.VMEM((SIDE, 2 * OWN, NSTATE), F32),
            pltpu.VMEM((SIDE, 2 * OWN, NSTATE), F32),
            pltpu.VMEM((SIDE, TOK, HDIM), F32),
            pltpu.VMEM((TOK, NSTATE), F32),
            pltpu.VMEM((TOK, NSTATE), F32),
            pltpu.VMEM((TOK, TOK), F32),
            pltpu.VMEM((8, wide), F32),
            pltpu.SemaphoreType.DMA((COPIES,)),
            pltpu.SemaphoreType.DMA((COPIES,)),
            pltpu.SemaphoreType.DMA((INPUTS,)),
            pltpu.SemaphoreType.DMA((len(outs),)),
        ],
        compiler_params=pltpu.CompilerParams(
            collective_id=0, has_side_effects=True, vmem_limit_bytes=60 << 20
        ),
    )(*inputs, skip)
    results = pl.pallas_call(
        hand_over,
        out_shape=outs,
        in_specs=in_place,
        out_specs=in_place,
        scratch_shapes=[pltpu.VMEM(a.shape, a.dtype) for a in outs]
        + [pltpu.SemaphoreType.DMA((len(outs),)), pltpu.SemaphoreType.DMA((len(outs),))],
        compiler_params=pltpu.CompilerParams(vmem_limit_bytes=60 << 20),
    )(*results)
    turn = (4, 6, 8)
    return tuple(r.T if i in turn else r for i, r in enumerate(results))


def solution(mesh):
    in_specs = (
        P("seq", "head"),
        P("seq", "head"),
        P("seq", "head"),
        P("seq", None),
        P("seq", None),
        P("seq", "head"),
        P(None, "head"),
        P("head"),
        P("head"),
        P("head", None),
        P(None, None, "head"),
        P("head", None),
        P(None, "head"),
        P("seq", "head"),
        P("seq", "head"),
    )
    out_specs = (
        P("seq", "head"),
        P("seq", "head"),
        P(("seq", "head"), None),
        P(("seq", "head"), None),
        P("seq", "head"),
        P("seq", "head"),
        P("head", None),
        P(None, None, "head"),
        P("head", None),
        P(None, "head"),
    )
    return jax.shard_map(body, mesh=mesh, in_specs=in_specs, out_specs=out_specs, check_vma=False)
```

```python
import jax
import jax.numpy as jnp
from jax import lax
from jax.experimental import pallas as pl
from jax.experimental.pallas import tpu as pltpu
from jax.sharding import PartitionSpec as P

ADAPTER_SCALE = 2.0
NORM_EPS = 1e-05
SIDE = 8
HDIM = 128
NSTATE = 128
TOK = 128
RANK = 32
KCONV = 4
OWN = TOK // SIDE
CHUNKS = 4
ROWS = NSTATE // CHUNKS
EARLY = 40
LATE = 24
MESH = pl.DeviceIdType.MESH
F32 = jnp.float32
BF16 = jnp.bfloat16


def own_place(kind):
    if kind == "head":
        return lax.axis_index("head")
    seq = lax.axis_index("seq")
    return lax.rem(seq, SIDE) if kind == "z" else seq // SIDE


def along(kind, step):
    if kind == "head":
        place = lax.rem(lax.axis_index("head") + step, SIDE)
        return {"head": place}, place
    seq = lax.axis_index("seq")
    if kind == "seq":
        place = lax.rem(seq + step + SIDE * SIDE, SIDE * SIDE)
        return {"seq": place}, place
    row, col = seq // SIDE, lax.rem(seq, SIDE)
    if kind == "z":
        place = lax.rem(col + step, SIDE)
        return {"seq": row * SIDE + place}, place
    place = lax.rem(row + step, SIDE)
    return {"seq": place * SIDE + col}, place


def send(device, source, target, send_sem, recv_sem):
    copy = pltpu.make_async_remote_copy(
        src_ref=source,
        dst_ref=target,
        send_sem=send_sem,
        recv_sem=recv_sem,
        device_id=device,
        device_id_type=MESH,
    )
    copy.start()
    return copy


FARTHEST = (4, 3, 5, 2, 6, 1, 7)


class Copies:
    def __init__(self, send_sem, recv_sem):
        self.send_sem, self.recv_sem, self.used, self.all = send_sem, recv_sem, 0, []

    def start(self, device, source, target):
        at = self.used
        self.used += 1
        copy = send(device, source, target, self.send_sem.at[at], self.recv_sem.at[at])
        self.all.append(copy)
        return copy

    def exchange(self, kind, source, target):
        started = {}
        for step in FARTHEST:
            device, place = along(kind, step)
            started[step] = self.start(device, source(place), target)
        return [started[step] for step in range(1, SIDE)]

    def left(self):
        for copy in self.all:
            copy.wait_send()


def arrived(copies):
    for copy in copies:
        copy.wait_recv()


def nn(a, b):
    return lax.dot_general(a, b, (((1,), (0,)), ((), ())), preferred_element_type=F32)


def nt(a, b):
    return lax.dot_general(a, b, (((1,), (1,)), ((), ())), preferred_element_type=F32)


def split(x):
    high = x.astype(BF16)
    return high, (x - high.astype(F32)).astype(BF16)


def left_exact(a, x, product=nn):
    high, low = split(x)
    return product(a, high) + product(a, low)


def right_exact(x, a, product=nn):
    high, low = split(x)
    return product(high, a) + product(low, a)


def both(x, y, product=nn):
    xh, xl = split(x)
    yh, yl = split(y)
    return product(xh, yh) + (product(xh, yl) + product(xl, yh))


def precise(a, b):
    return lax.dot_general(
        a, b, (((1,), (0,)), ((), ())), precision=lax.Precision.HIGHEST, preferred_element_type=F32
    )


def turned(x):
    missing = 128 - x.shape[1]
    if missing:
        x = jnp.concatenate([x, jnp.zeros((x.shape[0], missing), F32)], axis=1)
    return x.T


def sigmoid(x):
    return 1.0 / (1.0 + jnp.exp(-x))


def lanes(h):
    return pl.ds(pl.multiple_of(h * HDIM, HDIM), HDIM)


def each_head(step):
    lax.fori_loop(0, SIDE, lambda h, c: (step(h), c)[1], 0)


class Fold:
    def __init__(self, copies, refs, reverse):
        self.copies = copies
        (
            self.own, self.row_in, self.row_out, self.row_mix, self.part_out, self.part_in,
            self.out,
        ) = refs
        self.order = list(range(SIDE))[::-1] if reverse else list(range(SIDE))
        self.row, self.col = own_place("y"), own_place("z")
        self.flight = [[] for _ in range(CHUNKS)]

    def to_owner(self, chunk, step):
        at = pl.ds(8 + ROWS * chunk, ROWS) if chunk else pl.ds(0, 8 + ROWS)
        if step == SIDE:
            self.row_in[self.col, at] = self.own[self.col, at]
            return
        device, place = along("z", step)
        self.flight[chunk].append(
            self.copies.start(device, self.own.at[place, at], self.row_in.at[self.col, at])
        )

    def to_column(self, chunk):
        arrived(self.flight[chunk])
        state = jnp.zeros((ROWS, HDIM), F32)
        total = jnp.zeros((8, HDIM), F32)
        for place in self.order:
            self.row_out[chunk, place] = state
            if chunk == 0:
                self.row_mix[place] = jnp.exp(total)
            step = self.row_in[place, 0:8]
            total = total + step
            state = (
                jnp.exp(step[0:1]) * state
                + self.row_in[place, 8 + ROWS * chunk : 8 + ROWS * (chunk + 1)]
            )
        self.part_out[chunk, 0:8] = total
        self.part_out[chunk, 8 : 8 + ROWS] = state
        self.flight[chunk] = self.copies.exchange(
            "y", lambda place: self.part_out.at[chunk], self.part_in.at[chunk, self.row]
        )
        self.part_in[chunk, self.row] = self.part_out[chunk]

    def to_all(self, chunk):
        arrived(self.flight[chunk])
        part = jnp.zeros((ROWS, HDIM), F32)
        enter = part
        for place in self.order:
            enter = jnp.where(self.row == place, part, enter)
            decay = jnp.exp(self.part_in[chunk, place, 0:1])
            part = decay * part + self.part_in[chunk, place, 8 : 8 + ROWS]
        for place in range(SIDE):
            self.row_out[chunk, place] = (
                self.row_out[chunk, place] + self.row_mix[place, 0:1] * enter
            )
        at = pl.ds(ROWS * chunk, ROWS)
        self.flight[chunk] = self.copies.exchange(
            "z", lambda place: self.row_out.at[chunk, place], self.out.at[self.col, at]
        )
        self.out[self.col, at] = self.row_out[chunk, self.col]

    def end(self, step):
        for flight in self.flight:
            if step:
                flight[step - 1].wait_recv()
        return lax.rem(self.col - step + SIDE, SIDE)


NEAREST = (0, 1, 7, 2, 6, 3, 5, 4)


def fold_scratch():
    return [
        pltpu.VMEM((SIDE, NSTATE + 8, HDIM), F32),
        pltpu.VMEM((SIDE, NSTATE + 8, HDIM), F32),
        pltpu.VMEM((CHUNKS, SIDE, ROWS, HDIM), F32),
        pltpu.VMEM((SIDE, 8, HDIM), F32),
        pltpu.VMEM((CHUNKS, ROWS + 8, HDIM), F32),
        pltpu.VMEM((CHUNKS, SIDE, ROWS + 8, HDIM), F32),
        pltpu.VMEM((SIDE, NSTATE, HDIM), F32),
    ]


class TokenSum:
    def __init__(self, copies, refs, first, second):
        self.copies, self.first, self.second = copies, first, second
        self.own, self.first_in, self.second_out, self.second_in, self.all = refs
        self.part, self.other = own_place(first), own_place(second)
        self.flight = []

    def to_owner(self, start, rows):
        at = pl.ds(start, rows)
        self.flight += self.copies.exchange(
            self.first, lambda place: self.own.at[place, at], self.first_in.at[self.part, at]
        )
        self.first_in[self.part, at] = self.own[self.part, at]

    def to_line(self):
        arrived(self.flight)
        self.second_out[...] = head_total(self.first_in)
        self.flight = self.copies.exchange(
            self.second, lambda place: self.second_out, self.second_in.at[self.other]
        )
        self.second_in[self.other] = self.second_out[...]

    def to_all(self):
        arrived(self.flight)
        self.all[self.part] = head_total(self.second_in)
        self.flight = self.copies.exchange(
            self.first, lambda place: self.all.at[self.part], self.all.at[self.part]
        )

    def end(self):
        arrived(self.flight)


def token_sum_scratch(rows):
    return [
        pltpu.VMEM((SIDE, rows, HDIM), F32),
        pltpu.VMEM((SIDE, rows, HDIM), F32),
        pltpu.VMEM((rows, HDIM), F32),
        pltpu.VMEM((SIDE, rows, HDIM), F32),
        pltpu.VMEM((SIDE, rows, HDIM), F32),
    ]


def head_total(ref):
    total = ref[0]
    for place in range(1, SIDE):
        total = total + ref[place]
    return total


COPIES = 2 + 2 * 3 * CHUNKS * 7 + 5 * 7 + 2 * 7 * 7
WIDE = 13
INPUTS = 14
FETCH_ORDER = (1, 5, 3, 6, 11, 12, 8, 0, 4, 2, 13, 10, 7, 9)


def kernel(*refs):
    refs = list(refs)

    def take(n):
        out = refs[:n]
        del refs[:n]
        return out

    sources = take(INPUTS)
    (skip_ref,) = take(1)
    targets = take(10)
    places = take(INPUTS)
    (x_ref, conv_ref, gate_ref, b_ref, c_ref, l_ref, tap_ref, gain_ref, down_in_ref, up_in_ref,
     down_out_ref, up_out_ref, og_ref, base_ref) = places
    results = take(10)
    (gconv_ref, ggate_ref, gb_ref, gc_ref, gl_ref, glayer_ref, ga_in_ref, gb_in_ref, ga_out_ref,
     gb_out_ref) = results
    fold_refs, back_refs = take(7), take(7)
    early_refs, late_refs = (take(5), take(5)), (take(5), take(5))
    (
        pre3, act3, slope3, y3, outer3, mix3, decay3, weighted3, gs3, dgs3, gssd3, ecum3, toend3,
    ) = take(WIDE)
    (ext, halo, gext, halo_g, first_own, first_all, mid_own, mid_all, out_own, out_all, low_own,
     low_all, bc_own, bc_all, dcum3, gc_acc, gb_acc, dg_acc, rim_own) = take(19)
    send_sem, recv_sem, load_sem, store_sem = take(4)

    stores = []

    def store(*done):
        for ref in done:
            i = next(i for i, result in enumerate(results) if result is ref)
            copy = pltpu.make_async_copy(ref, targets[i], store_sem.at[i])
            copy.start()
            stores.append(copy)

    seq, head = lax.axis_index("seq"), lax.axis_index("head")
    copies = Copies(send_sem, recv_sem)
    barrier = pltpu.get_barrier_semaphore()
    greeted = 0
    for kind, steps in (
        ("seq", (1, -1)), ("z", range(1, SIDE)), ("y", range(1, SIDE)), ("head", range(1, SIDE))
    ):
        for step in steps:
            pl.semaphore_signal(
                barrier, inc=1, device_id=along(kind, step)[0], device_id_type=MESH
            )
            greeted += 1
    loads = {}
    for i in FETCH_ORDER:
        loads[i] = pltpu.make_async_copy(sources[i], places[i], load_sem.at[i])
        loads[i].start()

    def fetched(*which):
        for ref in which:
            loads[next(i for i, place in enumerate(places) if place is ref)].wait()

    fetched(conv_ref)
    ext[0:8] = jnp.zeros((8, SIDE * HDIM), F32)
    ext[8 : TOK + 8] = conv_ref[...].astype(F32)
    rows_at = lax.broadcasted_iota(jnp.int32, (TOK, TOK), 0)
    cols_at = lax.broadcasted_iota(jnp.int32, (TOK, TOK), 1)
    causal = rows_at >= cols_at
    fetched(l_ref, b_ref, tap_ref)
    cum_turned = precise(l_ref[...], (rows_at <= cols_at).astype(F32))
    cum = turned(jnp.concatenate([cum_turned, jnp.zeros((TOK - SIDE, TOK), F32)], axis=0))
    for h in range(SIDE):
        last = cum[TOK - 1 : TOK, h : h + 1]
        toend3[h] = jnp.exp(jnp.broadcast_to(last - cum[:, h : h + 1], (TOK, TOK)))
        total = jnp.broadcast_to(last, (8, HDIM))
        fold_refs[0][h, 0:8] = total
        back_refs[0][h, 0:8] = total
    b_turned = b_ref[...].astype(F32).T.astype(BF16)
    fold = Fold(copies, fold_refs, False)

    def activate(h, rows):
        at = lanes(h)
        taps = tap_ref[:, at].astype(F32)
        pre = ext[5 : 5 + rows, at] * taps[0:1]
        for k in range(1, KCONV):
            pre = pre + ext[5 + k : 5 + k + rows, at] * taps[k : k + 1]
        sig = sigmoid(pre)
        act3[h, 0:rows] = pre * sig
        slope3[h, 0:rows] = sig * (1.0 + pre * (1.0 - sig))

    each_head(lambda h: activate(h, TOK))
    pl.semaphore_wait(barrier, greeted)
    tail = copies.start(along("seq", 1)[0], conv_ref.at[TOK - 16 : TOK], halo)
    tail.wait_recv()
    ext[0:8] = jnp.where(seq > 0, halo[...].astype(F32)[8:16], 0.0)

    def local_state(h):
        activate(h, 8)
        fold.own[h, 8 : 8 + NSTATE] = left_exact(b_turned, act3[h] * toend3[h])

    for step in FARTHEST + (SIDE,):
        local_state(lax.rem(fold.col + step, SIDE))
        fold.to_owner(0, step)
    for chunk in range(1, CHUNKS):
        for step in FARTHEST + (SIDE,):
            fold.to_owner(chunk, step)

    fetched(up_out_ref, og_ref, down_in_ref, x_ref)
    first_own[0:RANK] = nt(up_out_ref[...], og_ref[...])
    first_own[RANK : 2 * RANK] = nt(down_in_ref[...], x_ref[...])
    first = copies.exchange("head", lambda place: first_own, first_all.at[head])
    first_all[head] = first_own[...]

    for h in range(SIDE):
        col = jnp.broadcast_to(cum[:, h : h + 1], (TOK, TOK))
        gap = col - cum_turned[h : h + 1]
        decay3[h] = jnp.where(causal, jnp.exp(jnp.where(causal, gap, 0.0)), 0.0)
        ecum3[h] = jnp.exp(col)
    fetched(c_ref, gate_ref)
    c_turned = c_ref[...].astype(F32).T.astype(BF16)
    scores = nt(c_ref[...], b_ref[...])
    scores_turned = nt(b_ref[...], c_ref[...])

    def inner(h):
        mix = decay3[h] * scores
        y3[h] = both(mix, act3[h]) + skip_ref[h] * act3[h]
        gate = gate_ref[:, lanes(h)].astype(F32)
        sig = sigmoid(gate)
        gs3[h] = gate * sig
        dgs3[h] = sig * (1.0 + gate * (1.0 - sig))

    fold.to_column(0)
    each_head(inner)
    fold.to_column(1)

    arrived(first)
    fetched(base_ref, down_out_ref, gain_ref, up_in_ref)
    sums = head_total(first_all)
    back_out_turned = sums[0:RANK]
    low_in_turned = sums[RANK : 2 * RANK]
    pad = jnp.zeros((TOK - RANK, TOK), F32)
    back_out = turned(jnp.concatenate([back_out_turned, pad], axis=0))[:, 0:RANK]

    def norm_gradient(h):
        at = lanes(h)
        weighted3[h] = (
            base_ref[:, at].astype(F32)
            + ADAPTER_SCALE * right_exact(back_out, down_out_ref[:, at])
        ) * gain_ref[:, at]

    each_head(norm_gradient)
    for chunk in range(2, CHUNKS):
        fold.to_column(chunk)
    for chunk in range(CHUNKS):
        fold.to_all(chunk)
    state_in = fold.out

    square, dot = jnp.zeros((TOK, HDIM), F32), jnp.zeros((TOK, HDIM), F32)
    for step in NEAREST:
        h = fold.end(step)
        outer = ecum3[h] * left_exact(c_ref[...], state_in[h])
        outer3[h] = outer
        y = y3[h] + outer
        y3[h] = y
        gated = y * gs3[h]
        square = square + gated * gated
        dot = dot + weighted3[h] * gated
    mid_own[...] = turned(
        jnp.concatenate(
            [
                jnp.sum(square, axis=1, keepdims=True),
                jnp.sum(dot, axis=1, keepdims=True),
                jnp.zeros((TOK, HDIM - 2), F32),
            ],
            axis=1,
        )
    )[0:8]
    mid = copies.exchange("head", lambda place: mid_own, mid_all.at[head])
    mid_all[head] = mid_own[...]

    def project(h, low):
        at = lanes(h)
        return low + left_exact(down_out_ref[:, at], y3[h] * gs3[h] * gain_ref[:, at], nt)

    out_own[...] = lax.fori_loop(0, SIDE, project, jnp.zeros((RANK, TOK), F32))
    out = copies.exchange("head", lambda place: out_own, out_all.at[head])
    out_all[head] = out_own[...]
    arrived(mid)
    sums = head_total(mid_all)
    inv_row = lax.rsqrt(sums[0:1] / (SIDE * SIDE * HDIM) + NORM_EPS)
    kappa_row = inv_row * inv_row * inv_row * sums[1:2] / (SIDE * SIDE * HDIM)
    columns = turned(
        jnp.concatenate([inv_row, kappa_row, jnp.zeros((TOK - 2, TOK), F32)], axis=0)
    )
    inv = jnp.broadcast_to(columns[:, 0:1], (TOK, HDIM))
    kappa = jnp.broadcast_to(columns[:, 1:2], (TOK, HDIM))

    def mixer_gradient(h):
        gated = y3[h] * gs3[h]
        grad_gated = inv * weighted3[h] - gated * kappa
        gssd = grad_gated * gs3[h]
        gssd3[h] = gssd
        pre3[h] = grad_gated * y3[h] * dgs3[h]
        back.own[h, 8 : 8 + NSTATE] = left_exact(c_turned, gssd * ecum3[h])

    back = Fold(copies, back_refs, True)
    for step in FARTHEST + (SIDE,):
        mixer_gradient(lax.rem(back.col + step, SIDE))
        back.to_owner(0, step)
    for chunk in range(1, CHUNKS):
        for step in FARTHEST + (SIDE,):
            back.to_owner(chunk, step)

    scale = ADAPTER_SCALE / (SIDE * SIDE * TOK)
    axes = (("z", "y"), ("y", "z"))
    early = [TokenSum(copies, refs, *axis) for refs, axis in zip(early_refs, axes)]

    def early_parts(h, low):
        at = lanes(h)
        ggate = pre3[h]
        ggate_ref[:, at] = ggate.astype(BF16)
        grad = scale * both(low_in_turned, ggate)
        early[0].own[h, 0:16] = grad[0:16]
        early[1].own[h, 0:16] = grad[16:32]
        normed = y3[h] * gs3[h] * gain_ref[:, at] * inv
        grad = scale * both(back_out_turned, normed)
        early[0].own[h, 16:32] = grad[0:16]
        early[1].own[h, 16:32] = grad[16:32]
        return low + left_exact(up_in_ref[1, :, at], ggate, nt)

    low_gate = lax.fori_loop(0, SIDE, early_parts, jnp.zeros((RANK, TOK), F32))
    arrived(out)
    low_out_turned = head_total(out_all) * inv_row
    grad_b_out = scale * right_exact(low_out_turned, og_ref[...])
    for part in range(SIDE):
        at = slice(HDIM * (part // 2), HDIM * (part // 2 + 1))
        for sums, first_row in zip(early, (8 * (part % 2), 16 + 8 * (part % 2))):
            sums.own[part, 32:40] = grad_b_out[first_row : first_row + 8, at]
    store(ggate_ref)
    for sums in early:
        sums.to_owner(0, EARLY)

    gc_acc[...] = jnp.zeros((TOK, NSTATE), F32)
    dg_acc[...] = jnp.zeros((TOK, TOK), F32)

    def local_gradient(h):
        gssd = gssd3[h]
        decay = decay3[h]
        part = both(gssd, act3[h], nt) * decay
        dg_acc[...] += part
        moved = part * scores
        dcum3[h] = moved - turned(moved) + gssd * outer3[h]
        mix3[h] = both(turned(decay) * scores_turned, gssd) + skip_ref[h] * gssd
        gc_acc[...] += both(gssd * ecum3[h], state_in[h], nt)

    lax.fori_loop(0, SIDE // 2, lambda h, c: (local_gradient(h), c)[1], 0)
    back.to_column(0)
    lax.fori_loop(SIDE // 2, SIDE, lambda h, c: (local_gradient(h), c)[1], 0)
    for chunk in range(1, CHUNKS):
        back.to_column(chunk)
    dg = dg_acc[...]
    gc_acc[...] += right_exact(dg, b_ref[...])
    gb_acc[...] = right_exact(turned(dg), c_ref[...])
    for chunk in range(CHUNKS - 1):
        back.to_all(chunk)
    back.to_all(CHUNKS - 1)
    for sums in early:
        sums.to_line()
    state_grad = back.out

    for step in NEAREST:
        h = back.end(step)
        into = toend3[h, 0:8] * left_exact(b_ref[0:16], state_grad[h])[0:8]
        rim_own[:, lanes(h)] = (mix3[h, 0:8] + into) * slope3[h, 0:8]
    rim = copies.start(along("seq", -1)[0], rim_own, halo_g)

    def state_gradient(h):
        toend = toend3[h]
        act = act3[h]
        into = toend * left_exact(b_ref[...], state_grad[h])
        gb_acc[...] += both(act * toend, state_grad[h], nt)
        fell = act * into
        total = jnp.sum(fell, axis=0, keepdims=True) + ecum3[h, TOK - 1 : TOK] * jnp.sum(
            state_in[h] * state_grad[h], axis=0, keepdims=True
        )
        dcum = dcum3[h] - fell
        dcum3[h] = jnp.where(rows_at == TOK - 1, dcum + total, dcum)
        gext[0:TOK, lanes(h)] = (mix3[h] + into) * slope3[h]

    each_head(state_gradient)
    for sums in early:
        sums.to_all()
    rim.wait_recv()
    gext[TOK : TOK + 8] = jnp.where(seq < SIDE * SIDE - 1, halo_g[...], 0.0)
    late = [TokenSum(copies, refs, *axis) for refs, axis in zip(late_refs, axes)]

    def conv_gradient(h, low):
        at = lanes(h)
        taps = tap_ref[:, at].astype(F32)
        gconv = gext[3 : 3 + TOK, at] * taps[0:1]
        for k in range(1, KCONV):
            gconv = gconv + gext[3 - k : 3 - k + TOK, at] * taps[k : k + 1]
        gconv_ref[:, at] = gconv.astype(BF16)
        y3[h] = gconv
        return low + left_exact(up_in_ref[0, :, at], gconv, nt)

    low_own[...] = lax.fori_loop(0, SIDE, conv_gradient, low_gate)
    low = copies.exchange("head", lambda place: low_own, low_all.at[head])
    low_all[head] = low_own[...]

    def conv_parts(h):
        grad = scale * both(low_in_turned, y3[h])
        late[0].own[h, 0:16] = grad[0:16]
        late[1].own[h, 0:16] = grad[16:32]

    each_head(conv_parts)
    for sums in late:
        sums.to_owner(0, 16)
    store(gconv_ref)
    dcum = turned(
        jnp.concatenate(
            [jnp.sum(dcum3[h], axis=1, keepdims=True) for h in range(SIDE)]
            + [jnp.zeros((TOK, HDIM - SIDE), F32)],
            axis=1,
        )
    )[0:SIDE]
    gl_ref[...] = precise(dcum, causal.astype(F32))
    store(gl_ref)
    arrived(low)
    back_in_turned = head_total(low_all)
    grad_a_in = scale * right_exact(back_in_turned, x_ref[...])
    for part in range(SIDE):
        at = slice(HDIM * (part // 2), HDIM * (part // 2 + 1))
        for sums, first_row in zip(late, (8 * (part % 2), 16 + 8 * (part % 2))):
            sums.own[part, 16:24] = grad_a_in[first_row : first_row + 8, at]
    for sums in late:
        sums.to_owner(16, 8)
    for part in range(SIDE):
        bc_own[part, 0:OWN] = gb_acc[OWN * part : OWN * (part + 1)]
        bc_own[part, OWN : 2 * OWN] = gc_acc[OWN * part : OWN * (part + 1)]
    rows_out = copies.exchange("head", lambda place: bc_own.at[place], bc_all.at[head])
    bc_all[head] = bc_own[head]
    back_in = turned(jnp.concatenate([back_in_turned, pad], axis=0))[:, 0:RANK]
    glayer_ref[...] = (ADAPTER_SCALE * right_exact(back_in, down_in_ref[...])).astype(BF16)
    for sums in late:
        sums.to_line()
    for sums in early:
        sums.end()
    for part in range(SIDE):
        at = slice(HDIM * part, HDIM * (part + 1))
        for half, sums in enumerate(early):
            rows = slice(16 * half, 16 * half + 16)
            gb_in_ref[1, rows, at] = sums.all[part, 0:16]
            ga_out_ref[rows, at] = sums.all[part, 16:32]
            first_row = 16 * half + 8 * (part % 2)
            gb_out_ref[
                first_row : first_row + 8, HDIM * (part // 2) : HDIM * (part // 2 + 1)
            ] = sums.all[part, 32:40]
    store(ga_out_ref, gb_out_ref)
    arrived(rows_out)
    sums = head_total(bc_all)
    gb_ref[...] = sums[0:OWN]
    gc_ref[...] = sums[OWN : 2 * OWN]
    store(glayer_ref, gb_ref, gc_ref)
    for sums in late:
        sums.to_all()
    for sums in late:
        sums.end()
    for part in range(SIDE):
        at = slice(HDIM * part, HDIM * (part + 1))
        gb_in_ref[0, 0:16, at] = late[0].all[part, 0:16]
        gb_in_ref[0, 16:32, at] = late[1].all[part, 0:16]
        at = slice(HDIM * (part // 2), HDIM * (part // 2 + 1))
        for sums, first_row in zip(late, (8 * (part % 2), 16 + 8 * (part % 2))):
            ga_in_ref[first_row : first_row + 8, at] = sums.all[part, 16:24]
    store(gb_in_ref, ga_in_ref)
    copies.left()
    for copy in stores:
        copy.wait()


def hand_over(*refs):
    count = (len(refs) - 2) // 3
    sources, targets, places = refs[:count], refs[count : 2 * count], refs[2 * count : 3 * count]
    load_sem, store_sem = refs[-2:]
    loads = [
        pltpu.make_async_copy(sources[i], places[i], load_sem.at[i]) for i in range(count)
    ]
    stores = [
        pltpu.make_async_copy(places[i], targets[i], store_sem.at[i]) for i in range(count)
    ]
    for load in loads:
        load.start()
    for load, store in zip(loads, stores):
        load.wait()
        store.start()
    for store in stores:
        store.wait()


def body(x, conv, gate, b, c, l, taps, skip, gain, down_in, up_in, down_out, up_out, og, base):
    wide = conv.shape[1]
    inputs = (
        x, conv, gate, b, c, l.T, taps, gain.reshape(1, wide), down_in.T, up_in, down_out.T,
        up_out, og, base,
    )
    outs = [
        jax.ShapeDtypeStruct(conv.shape, BF16),
        jax.ShapeDtypeStruct(gate.shape, BF16),
        jax.ShapeDtypeStruct((OWN, NSTATE), F32),
        jax.ShapeDtypeStruct((OWN, NSTATE), F32),
        jax.ShapeDtypeStruct(l.shape[::-1], F32),
        jax.ShapeDtypeStruct(x.shape, BF16),
        jax.ShapeDtypeStruct(down_in.shape[::-1], F32),
        jax.ShapeDtypeStruct(up_in.shape, F32),
        jax.ShapeDtypeStruct(down_out.shape[::-1], F32),
        jax.ShapeDtypeStruct(up_out.shape, F32),
    ]
    in_place = [pl.BlockSpec(memory_space=pl.ANY) for _ in outs]
    results = pl.pallas_call(
        kernel,
        out_shape=outs,
        in_specs=[pl.BlockSpec(memory_space=pl.ANY) for _ in inputs]
        + [pl.BlockSpec(memory_space=pltpu.SMEM)],
        out_specs=in_place,
        scratch_shapes=[pltpu.VMEM(a.shape, a.dtype) for a in inputs]
        + [pltpu.VMEM(a.shape, a.dtype) for a in outs]
        + fold_scratch()
        + fold_scratch()
        + token_sum_scratch(EARLY)
        + token_sum_scratch(EARLY)
        + token_sum_scratch(LATE)
        + token_sum_scratch(LATE)
        + [pltpu.VMEM((SIDE, TOK, HDIM), F32) for _ in range(WIDE)]
        + [
            pltpu.VMEM((TOK + 8, wide), F32),
            pltpu.VMEM((16, wide), BF16),
            pltpu.VMEM((TOK + 8, wide), F32),
            pltpu.VMEM((8, wide), F32),
            pltpu.VMEM((2 * RANK, TOK), F32),
            pltpu.VMEM((SIDE, 2 * RANK, TOK), F32),
            pltpu.VMEM((8, TOK), F32),
            pltpu.VMEM((SIDE, 8, TOK), F32),
            pltpu.VMEM((RANK, TOK), F32),
            pltpu.VMEM((SIDE, RANK, TOK), F32),
            pltpu.VMEM((RANK, TOK), F32),
            pltpu.VMEM((SIDE, RANK, TOK), F32),
            pltpu.VMEM((SIDE, 2 * OWN, NSTATE), F32),
            pltpu.VMEM((SIDE, 2 * OWN, NSTATE), F32),
            pltpu.VMEM((SIDE, TOK, HDIM), F32),
            pltpu.VMEM((TOK, NSTATE), F32),
            pltpu.VMEM((TOK, NSTATE), F32),
            pltpu.VMEM((TOK, TOK), F32),
            pltpu.VMEM((8, wide), F32),
            pltpu.SemaphoreType.DMA((COPIES,)),
            pltpu.SemaphoreType.DMA((COPIES,)),
            pltpu.SemaphoreType.DMA((INPUTS,)),
            pltpu.SemaphoreType.DMA((len(outs),)),
        ],
        compiler_params=pltpu.CompilerParams(
            collective_id=0, has_side_effects=True, vmem_limit_bytes=60 << 20
        ),
    )(*inputs, skip)
    results = pl.pallas_call(
        hand_over,
        out_shape=outs,
        in_specs=in_place,
        out_specs=in_place,
        scratch_shapes=[pltpu.VMEM(a.shape, a.dtype) for a in outs]
        + [pltpu.SemaphoreType.DMA((len(outs),)), pltpu.SemaphoreType.DMA((len(outs),))],
        compiler_params=pltpu.CompilerParams(vmem_limit_bytes=60 << 20),
    )(*results)
    turn = (4, 6, 8)
    return tuple(r.T if i in turn else r for i, r in enumerate(results))


def solution(mesh):
    in_specs = (
        P("seq", "head"),
        P("seq", "head"),
        P("seq", "head"),
        P("seq", None),
        P("seq", None),
        P("seq", "head"),
        P(None, "head"),
        P("head"),
        P("head"),
        P("head", None),
        P(None, None, "head"),
        P("head", None),
        P(None, "head"),
        P("seq", "head"),
        P("seq", "head"),
    )
    out_specs = (
        P("seq", "head"),
        P("seq", "head"),
        P(("seq", "head"), None),
        P(("seq", "head"), None),
        P("seq", "head"),
        P("seq", "head"),
        P("head", None),
        P(None, None, "head"),
        P("head", None),
        P(None, "head"),
    )
    return jax.shard_map(body, mesh=mesh, in_specs=in_specs, out_specs=out_specs, check_vma=False)
```

```python
import jax
import jax.numpy as jnp
from jax import lax
from jax.experimental import pallas as pl
from jax.experimental.pallas import tpu as pltpu
from jax.sharding import PartitionSpec as P

ADAPTER_SCALE = 2.0
NORM_EPS = 1e-05
SIDE = 8
HDIM = 128
NSTATE = 128
TOK = 128
RANK = 32
KCONV = 4
OWN = TOK // SIDE
CHUNKS = 4
ROWS = NSTATE // CHUNKS
EARLY = 40
LATE = 24
MESH = pl.DeviceIdType.MESH
F32 = jnp.float32
BF16 = jnp.bfloat16


def own_place(kind):
    if kind == "head":
        return lax.axis_index("head")
    seq = lax.axis_index("seq")
    return lax.rem(seq, SIDE) if kind == "z" else seq // SIDE


def along(kind, step):
    if kind == "head":
        place = lax.rem(lax.axis_index("head") + step, SIDE)
        return {"head": place}, place
    seq = lax.axis_index("seq")
    if kind == "seq":
        place = lax.rem(seq + step + SIDE * SIDE, SIDE * SIDE)
        return {"seq": place}, place
    row, col = seq // SIDE, lax.rem(seq, SIDE)
    if kind == "z":
        place = lax.rem(col + step, SIDE)
        return {"seq": row * SIDE + place}, place
    place = lax.rem(row + step, SIDE)
    return {"seq": place * SIDE + col}, place


def send(device, source, target, send_sem, recv_sem):
    copy = pltpu.make_async_remote_copy(
        src_ref=source,
        dst_ref=target,
        send_sem=send_sem,
        recv_sem=recv_sem,
        device_id=device,
        device_id_type=MESH,
    )
    copy.start()
    return copy


FARTHEST = (4, 3, 5, 2, 6, 1, 7)


class Copies:
    def __init__(self, send_sem, recv_sem):
        self.send_sem, self.recv_sem, self.used, self.all = send_sem, recv_sem, 0, []

    def start(self, device, source, target):
        at = self.used
        self.used += 1
        copy = send(device, source, target, self.send_sem.at[at], self.recv_sem.at[at])
        self.all.append(copy)
        return copy

    def exchange(self, kind, source, target):
        started = {}
        for step in FARTHEST:
            device, place = along(kind, step)
            started[step] = self.start(device, source(place), target)
        return [started[step] for step in range(1, SIDE)]

    def left(self):
        for copy in self.all:
            copy.wait_send()


def arrived(copies):
    for copy in copies:
        copy.wait_recv()


def nn(a, b):
    return lax.dot_general(a, b, (((1,), (0,)), ((), ())), preferred_element_type=F32)


def nt(a, b):
    return lax.dot_general(a, b, (((1,), (1,)), ((), ())), preferred_element_type=F32)


def split(x):
    high = x.astype(BF16)
    return high, (x - high.astype(F32)).astype(BF16)


def left_exact(a, x, product=nn):
    high, low = split(x)
    return product(a, high) + product(a, low)


def right_exact(x, a, product=nn):
    high, low = split(x)
    return product(high, a) + product(low, a)


def both(x, y, product=nn):
    xh, xl = split(x)
    yh, yl = split(y)
    return product(xh, yh) + (product(xh, yl) + product(xl, yh))


def precise(a, b):
    return lax.dot_general(
        a, b, (((1,), (0,)), ((), ())), precision=lax.Precision.HIGHEST, preferred_element_type=F32
    )


def turned(x):
    missing = 128 - x.shape[1]
    if missing:
        x = jnp.concatenate([x, jnp.zeros((x.shape[0], missing), F32)], axis=1)
    return x.T


def sigmoid(x):
    return 1.0 / (1.0 + jnp.exp(-x))


def lanes(h):
    return pl.ds(pl.multiple_of(h * HDIM, HDIM), HDIM)


def each_head(step):
    lax.fori_loop(0, SIDE, lambda h, c: (step(h), c)[1], 0)


class Fold:
    def __init__(self, copies, refs, reverse):
        self.copies = copies
        (
            self.own, self.row_in, self.row_out, self.row_mix, self.part_out, self.part_in,
            self.out,
        ) = refs
        self.order = list(range(SIDE))[::-1] if reverse else list(range(SIDE))
        self.row, self.col = own_place("y"), own_place("z")
        self.flight = [[] for _ in range(CHUNKS)]

    def to_owner(self, chunk, step):
        at = pl.ds(8 + ROWS * chunk, ROWS) if chunk else pl.ds(0, 8 + ROWS)
        if step == SIDE:
            self.row_in[self.col, at] = self.own[self.col, at]
            return
        device, place = along("z", step)
        self.flight[chunk].append(
            self.copies.start(device, self.own.at[place, at], self.row_in.at[self.col, at])
        )

    def to_column(self, chunk):
        arrived(self.flight[chunk])
        state = jnp.zeros((ROWS, HDIM), F32)
        total = jnp.zeros((8, HDIM), F32)
        for place in self.order:
            self.row_out[chunk, place] = state
            if chunk == 0:
                self.row_mix[place] = jnp.exp(total)
            step = self.row_in[place, 0:8]
            total = total + step
            state = (
                jnp.exp(step[0:1]) * state
                + self.row_in[place, 8 + ROWS * chunk : 8 + ROWS * (chunk + 1)]
            )
        self.part_out[chunk, 0:8] = total
        self.part_out[chunk, 8 : 8 + ROWS] = state
        self.flight[chunk] = self.copies.exchange(
            "y", lambda place: self.part_out.at[chunk], self.part_in.at[chunk, self.row]
        )
        self.part_in[chunk, self.row] = self.part_out[chunk]

    def to_all(self, chunk):
        arrived(self.flight[chunk])
        part = jnp.zeros((ROWS, HDIM), F32)
        enter = part
        for place in self.order:
            enter = jnp.where(self.row == place, part, enter)
            decay = jnp.exp(self.part_in[chunk, place, 0:1])
            part = decay * part + self.part_in[chunk, place, 8 : 8 + ROWS]
        for place in range(SIDE):
            self.row_out[chunk, place] = (
                self.row_out[chunk, place] + self.row_mix[place, 0:1] * enter
            )
        at = pl.ds(ROWS * chunk, ROWS)
        self.flight[chunk] = self.copies.exchange(
            "z", lambda place: self.row_out.at[chunk, place], self.out.at[self.col, at]
        )
        self.out[self.col, at] = self.row_out[chunk, self.col]

    def end(self, step):
        for flight in self.flight:
            if step:
                flight[step - 1].wait_recv()
        return lax.rem(self.col - step + SIDE, SIDE)


NEAREST = (0, 1, 7, 2, 6, 3, 5, 4)


def fold_scratch():
    return [
        pltpu.VMEM((SIDE, NSTATE + 8, HDIM), F32),
        pltpu.VMEM((SIDE, NSTATE + 8, HDIM), F32),
        pltpu.VMEM((CHUNKS, SIDE, ROWS, HDIM), F32),
        pltpu.VMEM((SIDE, 8, HDIM), F32),
        pltpu.VMEM((CHUNKS, ROWS + 8, HDIM), F32),
        pltpu.VMEM((CHUNKS, SIDE, ROWS + 8, HDIM), F32),
        pltpu.VMEM((SIDE, NSTATE, HDIM), F32),
    ]


class TokenSum:
    def __init__(self, copies, refs, first, second):
        self.copies, self.first, self.second = copies, first, second
        self.own, self.first_in, self.second_out, self.second_in, self.all = refs
        self.part, self.other = own_place(first), own_place(second)
        self.flight = []

    def to_owner(self, start, rows):
        at = pl.ds(start, rows)
        self.flight += self.copies.exchange(
            self.first, lambda place: self.own.at[place, at], self.first_in.at[self.part, at]
        )
        self.first_in[self.part, at] = self.own[self.part, at]

    def to_line(self):
        arrived(self.flight)
        self.second_out[...] = head_total(self.first_in)
        self.flight = self.copies.exchange(
            self.second, lambda place: self.second_out, self.second_in.at[self.other]
        )
        self.second_in[self.other] = self.second_out[...]

    def to_all(self):
        arrived(self.flight)
        self.all[self.part] = head_total(self.second_in)
        self.flight = self.copies.exchange(
            self.first, lambda place: self.all.at[self.part], self.all.at[self.part]
        )

    def end(self):
        arrived(self.flight)


def token_sum_scratch(rows):
    return [
        pltpu.VMEM((SIDE, rows, HDIM), F32),
        pltpu.VMEM((SIDE, rows, HDIM), F32),
        pltpu.VMEM((rows, HDIM), F32),
        pltpu.VMEM((SIDE, rows, HDIM), F32),
        pltpu.VMEM((SIDE, rows, HDIM), F32),
    ]


def head_total(ref):
    total = ref[0]
    for place in range(1, SIDE):
        total = total + ref[place]
    return total


COPIES = 2 + 2 * 3 * CHUNKS * 7 + 5 * 7 + 2 * 7 * 7
WIDE = 13
INPUTS = 14
FETCH_ORDER = (1, 5, 3, 6, 11, 12, 8, 0, 4, 2, 13, 10, 7, 9)


def kernel(*refs):
    refs = list(refs)

    def take(n):
        out = refs[:n]
        del refs[:n]
        return out

    sources = take(INPUTS)
    (skip_ref,) = take(1)
    targets = take(10)
    places = take(INPUTS)
    (x_ref, conv_ref, gate_ref, b_ref, c_ref, l_ref, tap_ref, gain_ref, down_in_ref, up_in_ref,
     down_out_ref, up_out_ref, og_ref, base_ref) = places
    results = take(10)
    (gconv_ref, ggate_ref, gb_ref, gc_ref, gl_ref, glayer_ref, ga_in_ref, gb_in_ref, ga_out_ref,
     gb_out_ref) = results
    fold_refs, back_refs = take(7), take(7)
    early_refs, late_refs = (take(5), take(5)), (take(5), take(5))
    (
        pre3, act3, slope3, y3, outer3, mix3, decay3, weighted3, gs3, dgs3, gssd3, ecum3, toend3,
    ) = take(WIDE)
    (ext, halo, gext, halo_g, first_own, first_all, mid_own, mid_all, out_own, out_all, low_own,
     low_all, bc_own, bc_all, dcum3, gc_acc, gb_acc, dg_acc, rim_own) = take(19)
    send_sem, recv_sem, load_sem, store_sem = take(4)

    stores = []

    def store(*done):
        for ref in done:
            i = next(i for i, result in enumerate(results) if result is ref)
            copy = pltpu.make_async_copy(ref, targets[i], store_sem.at[i])
            copy.start()
            stores.append(copy)

    seq, head = lax.axis_index("seq"), lax.axis_index("head")
    copies = Copies(send_sem, recv_sem)
    barrier = pltpu.get_barrier_semaphore()
    greeted = 0
    for kind, steps in (
        ("seq", (1, -1)), ("z", range(1, SIDE)), ("y", range(1, SIDE)), ("head", range(1, SIDE))
    ):
        for step in steps:
            pl.semaphore_signal(
                barrier, inc=1, device_id=along(kind, step)[0], device_id_type=MESH
            )
            greeted += 1
    loads = {}
    for i in FETCH_ORDER:
        loads[i] = pltpu.make_async_copy(sources[i], places[i], load_sem.at[i])
        loads[i].start()

    def fetched(*which):
        for ref in which:
            loads[next(i for i, place in enumerate(places) if place is ref)].wait()

    fetched(conv_ref)
    ext[0:8] = jnp.zeros((8, SIDE * HDIM), F32)
    ext[8 : TOK + 8] = conv_ref[...].astype(F32)
    rows_at = lax.broadcasted_iota(jnp.int32, (TOK, TOK), 0)
    cols_at = lax.broadcasted_iota(jnp.int32, (TOK, TOK), 1)
    causal = rows_at >= cols_at
    fetched(l_ref, b_ref, tap_ref)
    cum_turned = precise(l_ref[...], (rows_at <= cols_at).astype(F32))
    cum = turned(jnp.concatenate([cum_turned, jnp.zeros((TOK - SIDE, TOK), F32)], axis=0))
    for h in range(SIDE):
        last = cum[TOK - 1 : TOK, h : h + 1]
        toend3[h] = jnp.exp(jnp.broadcast_to(last - cum[:, h : h + 1], (TOK, TOK)))
        total = jnp.broadcast_to(last, (8, HDIM))
        fold_refs[0][h, 0:8] = total
        back_refs[0][h, 0:8] = total
    b_turned = b_ref[...].astype(F32).T.astype(BF16)
    fold = Fold(copies, fold_refs, False)

    def activate(h, rows):
        at = lanes(h)
        taps = tap_ref[:, at].astype(F32)
        pre = ext[5 : 5 + rows, at] * taps[0:1]
        for k in range(1, KCONV):
            pre = pre + ext[5 + k : 5 + k + rows, at] * taps[k : k + 1]
        sig = sigmoid(pre)
        act3[h, 0:rows] = pre * sig
        slope3[h, 0:rows] = sig * (1.0 + pre * (1.0 - sig))

    each_head(lambda h: activate(h, TOK))
    pl.semaphore_wait(barrier, greeted)
    tail = copies.start(along("seq", 1)[0], conv_ref.at[TOK - 16 : TOK], halo)
    tail.wait_recv()
    ext[0:8] = jnp.where(seq > 0, halo[...].astype(F32)[8:16], 0.0)

    def local_state(h):
        activate(h, 8)
        fold.own[h, 8 : 8 + NSTATE] = left_exact(b_turned, act3[h] * toend3[h])

    for step in FARTHEST + (SIDE,):
        local_state(lax.rem(fold.col + step, SIDE))
        fold.to_owner(0, step)
    for chunk in range(1, CHUNKS):
        for step in FARTHEST + (SIDE,):
            fold.to_owner(chunk, step)

    fetched(up_out_ref, og_ref, down_in_ref, x_ref)
    first_own[0:RANK] = nt(up_out_ref[...], og_ref[...])
    first_own[RANK : 2 * RANK] = nt(down_in_ref[...], x_ref[...])
    first = copies.exchange("head", lambda place: first_own, first_all.at[head])
    first_all[head] = first_own[...]

    for h in range(SIDE):
        col = jnp.broadcast_to(cum[:, h : h + 1], (TOK, TOK))
        gap = col - cum_turned[h : h + 1]
        decay3[h] = jnp.where(causal, jnp.exp(jnp.where(causal, gap, 0.0)), 0.0)
        ecum3[h] = jnp.exp(col)
    fetched(c_ref, gate_ref)
    c_turned = c_ref[...].astype(F32).T.astype(BF16)
    scores = nt(c_ref[...], b_ref[...])
    scores_turned = nt(b_ref[...], c_ref[...])

    def inner(h):
        mix = decay3[h] * scores
        y3[h] = both(mix, act3[h]) + skip_ref[h] * act3[h]
        gate = gate_ref[:, lanes(h)].astype(F32)
        sig = sigmoid(gate)
        gs3[h] = gate * sig
        dgs3[h] = sig * (1.0 + gate * (1.0 - sig))

    fold.to_column(0)
    each_head(inner)
    fold.to_column(1)

    arrived(first)
    fetched(base_ref, down_out_ref, gain_ref, up_in_ref)
    sums = head_total(first_all)
    back_out_turned = sums[0:RANK]
    low_in_turned = sums[RANK : 2 * RANK]
    pad = jnp.zeros((TOK - RANK, TOK), F32)
    back_out = turned(jnp.concatenate([back_out_turned, pad], axis=0))[:, 0:RANK]

    def norm_gradient(h):
        at = lanes(h)
        weighted3[h] = (
            base_ref[:, at].astype(F32)
            + ADAPTER_SCALE * right_exact(back_out, down_out_ref[:, at])
        ) * gain_ref[:, at]

    each_head(norm_gradient)
    for chunk in range(2, CHUNKS):
        fold.to_column(chunk)
    for chunk in range(CHUNKS):
        fold.to_all(chunk)
    state_in = fold.out

    square, dot = jnp.zeros((TOK, HDIM), F32), jnp.zeros((TOK, HDIM), F32)
    for step in NEAREST:
        h = fold.end(step)
        outer = ecum3[h] * left_exact(c_ref[...], state_in[h])
        outer3[h] = outer
        y = y3[h] + outer
        y3[h] = y
        gated = y * gs3[h]
        square = square + gated * gated
        dot = dot + weighted3[h] * gated
    mid_own[...] = turned(
        jnp.concatenate(
            [
                jnp.sum(square, axis=1, keepdims=True),
                jnp.sum(dot, axis=1, keepdims=True),
                jnp.zeros((TOK, HDIM - 2), F32),
            ],
            axis=1,
        )
    )[0:8]
    mid = copies.exchange("head", lambda place: mid_own, mid_all.at[head])
    mid_all[head] = mid_own[...]

    def project(h, low):
        at = lanes(h)
        return low + left_exact(down_out_ref[:, at], y3[h] * gs3[h] * gain_ref[:, at], nt)

    out_own[...] = lax.fori_loop(0, SIDE, project, jnp.zeros((RANK, TOK), F32))
    out = copies.exchange("head", lambda place: out_own, out_all.at[head])
    out_all[head] = out_own[...]
    arrived(mid)
    sums = head_total(mid_all)
    inv_row = lax.rsqrt(sums[0:1] / (SIDE * SIDE * HDIM) + NORM_EPS)
    kappa_row = inv_row * inv_row * inv_row * sums[1:2] / (SIDE * SIDE * HDIM)
    columns = turned(
        jnp.concatenate([inv_row, kappa_row, jnp.zeros((TOK - 2, TOK), F32)], axis=0)
    )
    inv = jnp.broadcast_to(columns[:, 0:1], (TOK, HDIM))
    kappa = jnp.broadcast_to(columns[:, 1:2], (TOK, HDIM))

    def mixer_gradient(h):
        gated = y3[h] * gs3[h]
        grad_gated = inv * weighted3[h] - gated * kappa
        gssd = grad_gated * gs3[h]
        gssd3[h] = gssd
        pre3[h] = grad_gated * y3[h] * dgs3[h]
        back.own[h, 8 : 8 + NSTATE] = left_exact(c_turned, gssd * ecum3[h])

    back = Fold(copies, back_refs, True)
    for step in FARTHEST + (SIDE,):
        mixer_gradient(lax.rem(back.col + step, SIDE))
        back.to_owner(0, step)
    for chunk in range(1, CHUNKS):
        for step in FARTHEST + (SIDE,):
            back.to_owner(chunk, step)

    scale = ADAPTER_SCALE / (SIDE * SIDE * TOK)
    axes = (("z", "y"), ("y", "z"))
    early = [TokenSum(copies, refs, *axis) for refs, axis in zip(early_refs, axes)]

    def early_parts(h, low):
        at = lanes(h)
        ggate = pre3[h]
        ggate_ref[:, at] = ggate.astype(BF16)
        grad = scale * both(low_in_turned, ggate)
        early[0].own[h, 0:16] = grad[0:16]
        early[1].own[h, 0:16] = grad[16:32]
        normed = y3[h] * gs3[h] * gain_ref[:, at] * inv
        grad = scale * both(back_out_turned, normed)
        early[0].own[h, 16:32] = grad[0:16]
        early[1].own[h, 16:32] = grad[16:32]
        return low + left_exact(up_in_ref[1, :, at], ggate, nt)

    low_gate = lax.fori_loop(0, SIDE, early_parts, jnp.zeros((RANK, TOK), F32))
    arrived(out)
    low_out_turned = head_total(out_all) * inv_row
    grad_b_out = scale * right_exact(low_out_turned, og_ref[...])
    for part in range(SIDE):
        at = slice(HDIM * (part // 2), HDIM * (part // 2 + 1))
        for sums, first_row in zip(early, (8 * (part % 2), 16 + 8 * (part % 2))):
            sums.own[part, 32:40] = grad_b_out[first_row : first_row + 8, at]
    store(ggate_ref)
    for sums in early:
        sums.to_owner(0, EARLY)

    gc_acc[...] = jnp.zeros((TOK, NSTATE), F32)
    dg_acc[...] = jnp.zeros((TOK, TOK), F32)

    def local_gradient(h):
        gssd = gssd3[h]
        decay = decay3[h]
        part = both(gssd, act3[h], nt) * decay
        dg_acc[...] += part
        moved = part * scores
        dcum3[h] = moved - turned(moved) + gssd * outer3[h]
        mix3[h] = both(turned(decay) * scores_turned, gssd) + skip_ref[h] * gssd
        gc_acc[...] += both(gssd * ecum3[h], state_in[h], nt)

    lax.fori_loop(0, SIDE // 2, lambda h, c: (local_gradient(h), c)[1], 0)
    back.to_column(0)
    lax.fori_loop(SIDE // 2, SIDE, lambda h, c: (local_gradient(h), c)[1], 0)
    for chunk in range(1, CHUNKS):
        back.to_column(chunk)
    dg = dg_acc[...]
    gc_acc[...] += right_exact(dg, b_ref[...])
    gb_acc[...] = right_exact(turned(dg), c_ref[...])
    for chunk in range(CHUNKS - 1):
        back.to_all(chunk)
    back.to_all(CHUNKS - 1)
    for sums in early:
        sums.to_line()
    state_grad = back.out

    for step in NEAREST:
        h = back.end(step)
        into = toend3[h, 0:8] * left_exact(b_ref[0:16], state_grad[h])[0:8]
        rim_own[:, lanes(h)] = (mix3[h, 0:8] + into) * slope3[h, 0:8]
    rim = copies.start(along("seq", -1)[0], rim_own, halo_g)

    def state_gradient(h):
        toend = toend3[h]
        act = act3[h]
        into = toend * left_exact(b_ref[...], state_grad[h])
        gb_acc[...] += both(act * toend, state_grad[h], nt)
        fell = act * into
        total = jnp.sum(fell, axis=0, keepdims=True) + ecum3[h, TOK - 1 : TOK] * jnp.sum(
            state_in[h] * state_grad[h], axis=0, keepdims=True
        )
        dcum = dcum3[h] - fell
        dcum3[h] = jnp.where(rows_at == TOK - 1, dcum + total, dcum)
        gext[0:TOK, lanes(h)] = (mix3[h] + into) * slope3[h]

    each_head(state_gradient)
    rim.wait_recv()
    gext[TOK : TOK + 8] = jnp.where(seq < SIDE * SIDE - 1, halo_g[...], 0.0)
    late = [TokenSum(copies, refs, *axis) for refs, axis in zip(late_refs, axes)]

    def conv_gradient(h, low):
        at = lanes(h)
        taps = tap_ref[:, at].astype(F32)
        gconv = gext[3 : 3 + TOK, at] * taps[0:1]
        for k in range(1, KCONV):
            gconv = gconv + gext[3 - k : 3 - k + TOK, at] * taps[k : k + 1]
        gconv_ref[:, at] = gconv.astype(BF16)
        y3[h] = gconv
        return low + left_exact(up_in_ref[0, :, at], gconv, nt)

    low_own[...] = lax.fori_loop(0, SIDE, conv_gradient, low_gate)
    low = copies.exchange("head", lambda place: low_own, low_all.at[head])
    low_all[head] = low_own[...]

    def conv_parts(h):
        grad = scale * both(low_in_turned, y3[h])
        late[0].own[h, 0:16] = grad[0:16]
        late[1].own[h, 0:16] = grad[16:32]

    each_head(conv_parts)
    for sums in late:
        sums.to_owner(0, 16)
    for sums in early:
        sums.to_all()
    store(gconv_ref)
    dcum = turned(
        jnp.concatenate(
            [jnp.sum(dcum3[h], axis=1, keepdims=True) for h in range(SIDE)]
            + [jnp.zeros((TOK, HDIM - SIDE), F32)],
            axis=1,
        )
    )[0:SIDE]
    gl_ref[...] = precise(dcum, causal.astype(F32))
    store(gl_ref)
    arrived(low)
    back_in_turned = head_total(low_all)
    grad_a_in = scale * right_exact(back_in_turned, x_ref[...])
    for part in range(SIDE):
        at = slice(HDIM * (part // 2), HDIM * (part // 2 + 1))
        for sums, first_row in zip(late, (8 * (part % 2), 16 + 8 * (part % 2))):
            sums.own[part, 16:24] = grad_a_in[first_row : first_row + 8, at]
    for sums in late:
        sums.to_owner(16, 8)
    for part in range(SIDE):
        bc_own[part, 0:OWN] = gb_acc[OWN * part : OWN * (part + 1)]
        bc_own[part, OWN : 2 * OWN] = gc_acc[OWN * part : OWN * (part + 1)]
    rows_out = copies.exchange("head", lambda place: bc_own.at[place], bc_all.at[head])
    bc_all[head] = bc_own[head]
    back_in = turned(jnp.concatenate([back_in_turned, pad], axis=0))[:, 0:RANK]
    glayer_ref[...] = (ADAPTER_SCALE * right_exact(back_in, down_in_ref[...])).astype(BF16)
    for sums in late:
        sums.to_line()
    for sums in early:
        sums.end()
    for part in range(SIDE):
        at = slice(HDIM * part, HDIM * (part + 1))
        for half, sums in enumerate(early):
            rows = slice(16 * half, 16 * half + 16)
            gb_in_ref[1, rows, at] = sums.all[part, 0:16]
            ga_out_ref[rows, at] = sums.all[part, 16:32]
            first_row = 16 * half + 8 * (part % 2)
            gb_out_ref[
                first_row : first_row + 8, HDIM * (part // 2) : HDIM * (part // 2 + 1)
            ] = sums.all[part, 32:40]
    store(ga_out_ref, gb_out_ref)
    arrived(rows_out)
    sums = head_total(bc_all)
    gb_ref[...] = sums[0:OWN]
    gc_ref[...] = sums[OWN : 2 * OWN]
    store(glayer_ref, gb_ref, gc_ref)
    for sums in late:
        sums.to_all()
    for sums in late:
        sums.end()
    for part in range(SIDE):
        at = slice(HDIM * part, HDIM * (part + 1))
        gb_in_ref[0, 0:16, at] = late[0].all[part, 0:16]
        gb_in_ref[0, 16:32, at] = late[1].all[part, 0:16]
        at = slice(HDIM * (part // 2), HDIM * (part // 2 + 1))
        for sums, first_row in zip(late, (8 * (part % 2), 16 + 8 * (part % 2))):
            ga_in_ref[first_row : first_row + 8, at] = sums.all[part, 16:24]
    store(gb_in_ref, ga_in_ref)
    copies.left()
    for copy in stores:
        copy.wait()


def hand_over(*refs):
    count = (len(refs) - 2) // 3
    sources, targets, places = refs[:count], refs[count : 2 * count], refs[2 * count : 3 * count]
    load_sem, store_sem = refs[-2:]
    loads = [
        pltpu.make_async_copy(sources[i], places[i], load_sem.at[i]) for i in range(count)
    ]
    stores = [
        pltpu.make_async_copy(places[i], targets[i], store_sem.at[i]) for i in range(count)
    ]
    for load in loads:
        load.start()
    for load, store in zip(loads, stores):
        load.wait()
        store.start()
    for store in stores:
        store.wait()


def body(x, conv, gate, b, c, l, taps, skip, gain, down_in, up_in, down_out, up_out, og, base):
    wide = conv.shape[1]
    inputs = (
        x, conv, gate, b, c, l.T, taps, gain.reshape(1, wide), down_in.T, up_in, down_out.T,
        up_out, og, base,
    )
    outs = [
        jax.ShapeDtypeStruct(conv.shape, BF16),
        jax.ShapeDtypeStruct(gate.shape, BF16),
        jax.ShapeDtypeStruct((OWN, NSTATE), F32),
        jax.ShapeDtypeStruct((OWN, NSTATE), F32),
        jax.ShapeDtypeStruct(l.shape[::-1], F32),
        jax.ShapeDtypeStruct(x.shape, BF16),
        jax.ShapeDtypeStruct(down_in.shape[::-1], F32),
        jax.ShapeDtypeStruct(up_in.shape, F32),
        jax.ShapeDtypeStruct(down_out.shape[::-1], F32),
        jax.ShapeDtypeStruct(up_out.shape, F32),
    ]
    in_place = [pl.BlockSpec(memory_space=pl.ANY) for _ in outs]
    results = pl.pallas_call(
        kernel,
        out_shape=outs,
        in_specs=[pl.BlockSpec(memory_space=pl.ANY) for _ in inputs]
        + [pl.BlockSpec(memory_space=pltpu.SMEM)],
        out_specs=in_place,
        scratch_shapes=[pltpu.VMEM(a.shape, a.dtype) for a in inputs]
        + [pltpu.VMEM(a.shape, a.dtype) for a in outs]
        + fold_scratch()
        + fold_scratch()
        + token_sum_scratch(EARLY)
        + token_sum_scratch(EARLY)
        + token_sum_scratch(LATE)
        + token_sum_scratch(LATE)
        + [pltpu.VMEM((SIDE, TOK, HDIM), F32) for _ in range(WIDE)]
        + [
            pltpu.VMEM((TOK + 8, wide), F32),
            pltpu.VMEM((16, wide), BF16),
            pltpu.VMEM((TOK + 8, wide), F32),
            pltpu.VMEM((8, wide), F32),
            pltpu.VMEM((2 * RANK, TOK), F32),
            pltpu.VMEM((SIDE, 2 * RANK, TOK), F32),
            pltpu.VMEM((8, TOK), F32),
            pltpu.VMEM((SIDE, 8, TOK), F32),
            pltpu.VMEM((RANK, TOK), F32),
            pltpu.VMEM((SIDE, RANK, TOK), F32),
            pltpu.VMEM((RANK, TOK), F32),
            pltpu.VMEM((SIDE, RANK, TOK), F32),
            pltpu.VMEM((SIDE, 2 * OWN, NSTATE), F32),
            pltpu.VMEM((SIDE, 2 * OWN, NSTATE), F32),
            pltpu.VMEM((SIDE, TOK, HDIM), F32),
            pltpu.VMEM((TOK, NSTATE), F32),
            pltpu.VMEM((TOK, NSTATE), F32),
            pltpu.VMEM((TOK, TOK), F32),
            pltpu.VMEM((8, wide), F32),
            pltpu.SemaphoreType.DMA((COPIES,)),
            pltpu.SemaphoreType.DMA((COPIES,)),
            pltpu.SemaphoreType.DMA((INPUTS,)),
            pltpu.SemaphoreType.DMA((len(outs),)),
        ],
        compiler_params=pltpu.CompilerParams(
            collective_id=0, has_side_effects=True, vmem_limit_bytes=60 << 20
        ),
    )(*inputs, skip)
    results = pl.pallas_call(
        hand_over,
        out_shape=outs,
        in_specs=in_place,
        out_specs=in_place,
        scratch_shapes=[pltpu.VMEM(a.shape, a.dtype) for a in outs]
        + [pltpu.SemaphoreType.DMA((len(outs),)), pltpu.SemaphoreType.DMA((len(outs),))],
        compiler_params=pltpu.CompilerParams(vmem_limit_bytes=60 << 20),
    )(*results)
    turn = (4, 6, 8)
    return tuple(r.T if i in turn else r for i, r in enumerate(results))


def solution(mesh):
    in_specs = (
        P("seq", "head"),
        P("seq", "head"),
        P("seq", "head"),
        P("seq", None),
        P("seq", None),
        P("seq", "head"),
        P(None, "head"),
        P("head"),
        P("head"),
        P("head", None),
        P(None, None, "head"),
        P("head", None),
        P(None, "head"),
        P("seq", "head"),
        P("seq", "head"),
    )
    out_specs = (
        P("seq", "head"),
        P("seq", "head"),
        P(("seq", "head"), None),
        P(("seq", "head"), None),
        P("seq", "head"),
        P("seq", "head"),
        P("head", None),
        P(None, None, "head"),
        P("head", None),
        P(None, "head"),
    )
    return jax.shard_map(body, mesh=mesh, in_specs=in_specs, out_specs=out_specs, check_vma=False)
```
